256 devices in a mesh: dp: 16 (over y, z_hi, core), tensor: 16 (over z_lo, x).
Axes of the slice: x: 4, y: 4, z: 8 (z_hi: 2, z_lo: 4; z = z_hi * 4 + z_lo), core: 2. Of those that a mesh axis runs over, the one named last changes fastest.
Arguments:
- tokens: bfloat16 [1024, 8192], P('tensor', 'dp'), may hold values from -6 to 6
- gate_weight: bfloat16 [8192, 29568], P('dp', 'tensor'), may hold values from -0.0625 to 0.0625
- up_weight: bfloat16 [8192, 29568], P('dp', 'tensor'), may hold values from -0.0625 to 0.0625
- down_weight: bfloat16 [29568, 8192], P('tensor', 'dp'), may hold values from -0.03125 to 0.03125
- labels: int32 [1024], P('tensor'), may hold values from 0 to 255
Outputs:
- erased: bfloat16 [1024, 8192], P('tensor', 'dp')
The draws below stay inside these ranges and needn't reach their ends.
All inputs are finite; a program needn't handle non-finite values.
Results may differ from the reference program's by a relative error of at most 0.029.
Values may be sent and summed in bfloat16 or wider, within the bound.
A program may use at most 64 MiB of HBM per device.

```python
import jax
import jax.numpy as jnp
from jax import lax

D = 8192
FF = 29568
NCLS = 256
TOKENS = 1024
DBLK = 512
N_DP = 16


def with_ends(array, rng, least, top_value):
    dims = array.shape
    place = [jax.random.randint(jax.random.fold_in(rng, axis), (), 0, dims[axis]) for axis in range(len(dims))]
    array = array.at[tuple(place)].set(least)
    longest = dims.index(max(dims))
    place[longest] = (place[longest] + 1) % dims[longest]
    return array.at[tuple(place)].set(top_value)


def shard_levels(stream_key, extent, cuts, low, largest):
    level, own = 1.0, jax.random.fold_in(stream_key, 6)
    for axis_at, shards_of in cuts:
        steps = jnp.exp(jax.random.uniform(jax.random.fold_in(own, axis_at), (shards_of,), jnp.float32, low / len(cuts), largest / len(cuts)))
        level = level * jnp.repeat(steps, extent[axis_at] // shards_of).reshape([-1 if axis == axis_at else 1 for axis in range(len(extent))])
    return level


def normal_values(rng, extent, width, bound, cuts=(), held_as=jnp.bfloat16):
    entries = jax.random.normal(rng, extent, jnp.float32) * width
    if len(cuts) > 0:
        entries = shard_levels(rng, extent, cuts, -0.22, 0.18) * entries
    return jnp.clip(entries, min=-bound, max=bound).astype(held_as)


def setup_inputs(seed: int = 0) -> dict:
    seeds = jax.random.split(jax.random.key(seed), 6)
    tokens = normal_values(seeds[0], (TOKENS, D), 1.0, 6.0, ((0, 16), (1, 16)))
    gate_weight = normal_values(seeds[1], (D, FF), D ** -0.5, 0.0625, ((0, 16), (1, 16)))
    up_weight = normal_values(seeds[2], (D, FF), D ** -0.5, 0.0625, ((0, 16), (1, 16)))
    down_weight = normal_values(seeds[3], (FF, D), FF ** -0.5, 0.03125, ((0, 16), (1, 16)))
    labels = with_ends(jax.random.randint(seeds[4], (TOKENS,), 0, NCLS), jax.random.fold_in(seeds[4], 1), 0, NCLS - 1).astype(jnp.int32)
    return dict(tokens=tokens, gate_weight=gate_weight, up_weight=up_weight, down_weight=down_weight, labels=labels)


epsilon = 1e-05
ridge_share = 0.5

def block_sum(tokens, weight):

    def step(running, block_index):
        slab_rows = lax.dynamic_slice_in_dim(tokens, block_index * DBLK, DBLK, 1)
        slab_cols = lax.dynamic_slice_in_dim(weight, block_index * DBLK, DBLK, 0)
        partial_value = jnp.dot(slab_rows.astype(jnp.float32), slab_cols.astype(jnp.float32), preferred_element_type=jnp.float32).astype(jnp.bfloat16)
        partial_value = lax.optimization_barrier(partial_value).astype(jnp.float32)
        return (running + partial_value, None)
    start_sum = jnp.zeros((tokens.shape[0], weight.shape[1]), jnp.float32)
    running, _ = lax.scan(step, start_sum, jnp.arange(N_DP, dtype=jnp.int32))
    return running

def reference(tokens, gate_weight, up_weight, down_weight, labels):
    gate = block_sum(tokens, gate_weight)
    up = block_sum(tokens, up_weight)
    hidden = (jax.nn.silu(gate) * up).astype(jnp.bfloat16)
    output = jnp.dot(hidden.astype(jnp.float32), down_weight.astype(jnp.float32), preferred_element_type=jnp.float32)
    classes = jnp.arange(NCLS, dtype=jnp.int32)
    onehot = (labels[:, None] == classes[None, :]).astype(jnp.float32)
    mean_out = lax.optimization_barrier(jnp.mean(output, axis=0))
    shares = lax.optimization_barrier(jnp.mean(onehot, axis=0))
    centred = output - mean_out
    high = lax.Precision.HIGHEST
    cross = jnp.dot(centred.T, onehot - shares, precision=high) / TOKENS
    variance = lax.optimization_barrier(jnp.mean(centred * centred, axis=0))
    spread = jnp.sqrt(variance + epsilon)
    whitened = cross / spread[:, None]
    gram_mat = jnp.dot(whitened.T, whitened, precision=high)
    ridge_term = ridge_share * jnp.trace(gram_mat) / NCLS
    factor = jnp.linalg.cholesky(gram_mat + ridge_term * jnp.eye(NCLS, dtype=jnp.float32))
    coords = jnp.dot(centred / spread, whitened, precision=high)
    solved = jax.scipy.linalg.cho_solve((factor, True), coords.T)
    correction = jnp.dot(whitened, solved, precision=high).T * spread
    return (output - correction).astype(jnp.bfloat16)
```

```python
import functools

import jax
import jax.numpy as jnp
from jax import lax
from jax.experimental import pallas as pl
from jax.experimental.pallas import tpu as pltpu
from jax.sharding import PartitionSpec as P

MESH = pl.DeviceIdType.MESH
NCLS = 256
TOKENS = 1024
UNITS = 928
SHIFT = 920
CHUNKS = (240, 240, 224, 224)
epsilon = 1e-05
ridge_share = 0.5
f32 = jnp.float32
bf16 = jnp.bfloat16
VM = pl.BlockSpec(memory_space=pltpu.VMEM)
ANY = pl.BlockSpec(memory_space=pl.ANY)


class Spot:
    def __init__(self):
        dp, tn = lax.axis_index("dp"), lax.axis_index("tensor")
        self.dp, self.tn = dp, tn
        self.core = lax.rem(dp, 2)
        self.zh = lax.rem(dp // 2, 2)
        self.y = dp // 4
        self.x = lax.rem(tn, 4)
        self.zl = tn // 4

    def dpid(self, y=None, zh=None, core=None):
        y = self.y if y is None else y
        zh = self.zh if zh is None else zh
        core = self.core if core is None else core
        return {"dp": y * 4 + zh * 2 + core}

    def tid(self, zl=None, x=None):
        zl = self.zl if zl is None else zl
        x = self.x if x is None else x
        return {"tensor": zl * 4 + x}


def up4(v, d):
    return lax.rem(v + d, 4)


def greet(peers):
    barrier = pltpu.get_barrier_semaphore()
    for peer in peers:
        pl.semaphore_signal(barrier, inc=1, device_id=peer, device_id_type=MESH)
    pl.semaphore_wait(barrier, len(peers))


def push(src, dst, ssem, rsem, dev):
    copy = pltpu.make_async_remote_copy(
        src_ref=src, dst_ref=dst, send_sem=ssem, recv_sem=rsem, device_id=dev, device_id_type=MESH
    )
    copy.start()
    return copy


def gather_tensor(me, parts):
    copies = []
    zc, rc, lc, fc = {}, {}, {}, {}
    right, left = up4(me.x, 1), up4(me.x, 3)
    for i, (own, block, ss, rs) in enumerate(parts):
        for d in (1, 2, 3):
            zc[i, d] = push(own, block(me.zl, me.x), ss.at[d], rs.at[d], me.tid(zl=up4(me.zl, d)))
    for d in range(4):
        z = up4(me.zl, 4 - d)
        for i, (own, block, ss, rs) in enumerate(parts):
            src = own
            if d:
                zc[i, d].wait_recv()
                src = block(z, me.x)
            rc[i, d] = push(src, block(z, me.x), ss.at[4 + d], rs.at[4 + d], me.tid(x=right))
            lc[i, d] = push(src, block(z, me.x), ss.at[8 + d], rs.at[8 + d], me.tid(x=left))
    for d in range(4):
        z = up4(me.zl, 4 - d)
        for i, (own, block, ss, rs) in enumerate(parts):
            rc[i, d].wait_recv()
            lc[i, d].wait_recv()
            if d < 2:
                v = block(z, left)
                fc[i, d] = push(v, v, ss.at[12 + d], rs.at[12 + d], me.tid(x=right))
            else:
                v = block(z, right)
                fc[i, d] = push(v, v, ss.at[12 + d], rs.at[12 + d], me.tid(x=left))
    for c in fc.values():
        c.wait_recv()
    return [*zc.values(), *rc.values(), *lc.values(), *fc.values()]


def tensor_peers(me):
    peers = [me.tid(zl=up4(me.zl, d)) for d in (1, 2, 3)]
    return peers + [me.tid(x=up4(me.x, 1)), me.tid(x=up4(me.x, 3))]


def nt(a, b):
    return lax.dot_general(a, b, (((1,), (1,)), ((), ())), preferred_element_type=f32)


def hidden_kernel(tok, lab, wg, wu, h, labs, T, Tp, W, S, R, K2, PO, SZ, RZ,
                  ts, tr, ls, lr, ws, wr, wl, cs, cr, rs, rr, zs, zr):
    me = Spot()
    other = 1 - me.core
    own_rows = pl.ds(pl.multiple_of(SHIFT * me.core, 8), UNITS)
    far_rows = pl.ds(pl.multiple_of(SHIFT * other, 8), UNITS)
    local = []
    for i, w in enumerate((wg, wu)):
        c = pltpu.make_async_copy(w.at[own_rows], W.at[0, i], wl.at[i])
        c.start()
        local.append(c)
    yr, yl = up4(me.y, 1), up4(me.y, 3)
    to_r, to_l = me.dpid(y=yr), me.dpid(y=yl)
    mate = me.dpid(core=other)
    greet(tensor_peers(me) + [to_r, to_l, me.dpid(zh=1 - me.zh), mate])
    sent = []
    wx = []
    for i, w in enumerate((wg, wu)):
        wx.append(push(w.at[far_rows], W.at[1, i], ws.at[i], wr.at[i], mate))

    def tblock(zl, x):
        return T.at[pl.ds(pl.multiple_of(64 * (4 * zl + x), 64), 64)]

    def lblock(zl, x):
        return labs.at[4 * zl + x]

    T[pl.ds(pl.multiple_of(64 * me.tn, 64), 64), :] = tok[...]
    labs[me.tn] = lab[...]
    sent += gather_tensor(me, [(tok, tblock, ts, tr), (lab, lblock, ls, lr)])
    order = (2, 1, 3, 0)
    tx = []
    for k, d in enumerate(order):
        rows = pl.ds(pl.multiple_of(256 * up4(me.y, d), 256), 256)
        tx.append(push(T.at[rows], Tp.at[rows], cs.at[k], cr.at[k], mate))
    for c in local:
        c.wait()
    for c in wx:
        c.wait_recv()
    for c in tx:
        c.wait_recv()
    sent += wx + tx

    starts = [sum(CHUNKS[:q]) for q in range(len(CHUNKS))]

    def mult(i, q, d):
        a, n = starts[q], CHUNKS[q]
        rows = pl.ds(pl.multiple_of(256 * up4(me.y, d), 256), 256)
        return nt(W[0, i, a:a + n, :], T[rows, :]) + nt(W[1, i, a:a + n, :], Tp[rows, :])

    cps = {}

    def send(k, q, dev):
        rows = pl.ds(2 * starts[q], 2 * CHUNKS[q])
        cps[k, q] = push(S.at[k, rows], R.at[k, rows], rs.at[k, q], rr.at[k, q], dev)

    def first(q):
        a, n = starts[q], CHUNKS[q]
        for i in range(2):
            o = 2 * a + i * n
            p = mult(i, q, 2)
            S[0, o:o + n, :] = p[:, :128].astype(bf16)
            S[1, o:o + n, :] = p[:, 128:].astype(bf16)
        send(0, q, to_r)
        send(1, q, to_l)
        for i in range(2):
            o = 2 * a + i * n
            p = mult(i, q, 1)
            K2[0, o:o + n, :] = p[:, :128]
            S[3, o:o + n, :] = p[:, 128:].astype(bf16)
        send(3, q, to_r)
        for i in range(2):
            o = 2 * a + i * n
            p = mult(i, q, 3)
            K2[1, o:o + n, :] = p[:, 128:]
            S[4, o:o + n, :] = p[:, :128].astype(bf16)
        send(4, q, to_l)
        for i in range(2):
            o = 2 * a + i * n
            PO[o:o + n, :] = mult(i, q, 0)

    def second(q):
        o, n = 2 * starts[q], 2 * CHUNKS[q]
        cps[0, q].wait_recv()
        S[2, o:o + n, :] = (K2[0, o:o + n, :] + R[0, o:o + n, :].astype(f32)).astype(bf16)
        send(2, q, to_r)
        cps[1, q].wait_recv()
        S[5, o:o + n, :] = (K2[1, o:o + n, :] + R[1, o:o + n, :].astype(f32)).astype(bf16)
        send(5, q, to_l)

    zc = {}

    def third(q):
        o, n = 2 * starts[q], 2 * CHUNKS[q]
        for k in (2, 3, 4, 5):
            cps[k, q].wait_recv()
        a = PO[o:o + n, :128] + R[2, o:o + n, :].astype(f32) + R[4, o:o + n, :].astype(f32)
        b = PO[o:o + n, 128:] + R[3, o:o + n, :].astype(f32) + R[5, o:o + n, :].astype(f32)
        low = me.zh == 0
        SZ[o:o + n, :] = jnp.where(low, b, a).astype(bf16)
        PO[o:o + n, :128] = jnp.where(low, a, b)
        rows = pl.ds(o, n)
        zc[q] = push(SZ.at[rows], RZ.at[rows], zs.at[q], zr.at[q], me.dpid(zh=1 - me.zh))

    def last(q):
        a, n = starts[q], CHUNKS[q]
        o = 2 * a
        zc[q].wait_recv()
        tot = PO[o:o + 2 * n, :128] + RZ[o:o + 2 * n, :].astype(f32)
        g, u = tot[:n], tot[n:]
        h[a:a + n, :] = (g / (1.0 + jnp.exp(-g)) * u).astype(bf16)

    nq = len(CHUNKS)
    for i in range(nq + 2):
        if i < nq:
            first(i)
        if 1 <= i <= nq:
            second(i - 1)
        if i >= 2:
            third(i - 2)
    for q in range(nq):
        last(q)
    for c in [*sent, *cps.values(), *zc.values()]:
        c.wait_send()


def down_kernel(h, down, outt, D, DT, H, PG, KO, SO, RO, SZ, RZ,
                dl, hs, hr, cs, cr, os, orr, zs, zr):
    me = Spot()
    other = 1 - me.core
    loads = []
    for i, c in enumerate((me.core, other)):
        cp = pltpu.make_async_copy(
            down.at[pl.ds(pl.multiple_of(SHIFT * c, 8), UNITS)], D.at[i, pl.ds(0, UNITS)], dl.at[i]
        )
        cp.start()
        loads.append(cp)
    yr, yl, yf = up4(me.y, 1), up4(me.y, 3), up4(me.y, 2)
    to_r, to_l = me.dpid(y=yr), me.dpid(y=yl)
    mate = me.dpid(core=other)
    across = me.dpid(zh=1 - me.zh)
    xr, xl = me.tid(x=up4(me.x, 1)), me.tid(x=up4(me.x, 3))
    greet(tensor_peers(me) + [to_r, to_l, across, mate])

    def hv(i, y, zh):
        return H.at[i, y, pl.ds(0, UNITS), pl.ds(pl.multiple_of(128 * zh, 128), 128)]

    zh, zo = me.zh, 1 - me.zh
    sent = []
    cc = {}

    def share(k, src, y, z):
        cc[k] = push(src, hv(1, y, z), cs.at[k], cr.at[k], mate)
        sent.append(cc[k])

    cz = push(h, hv(0, me.y, zh), hs.at[0], hr.at[0], across)
    cr0 = push(h, hv(0, me.y, zh), hs.at[1], hr.at[1], to_r)
    cl0 = push(h, hv(0, me.y, zh), hs.at[2], hr.at[2], to_l)
    share(0, h, me.y, zh)
    H[0, me.y, 0:UNITS, pl.ds(pl.multiple_of(128 * zh, 128), 128)] = h[...]
    H[:, :, UNITS:, :] = jnp.zeros((2, 4, 1024 - UNITS, 256), bf16)
    for i in range(2):
        loads[i].wait()
        D[i, UNITS:, :] = jnp.zeros((1024 - UNITS, 512), bf16)
        dup = (me.core if i == 0 else other) == 1
        head = D[i, 0:16, :].astype(f32)
        row = lax.broadcasted_iota(jnp.int32, head.shape, 0)
        D[i, 0:16, :] = jnp.where(jnp.logical_and(dup, row < 8), 0.0, head).astype(bf16)
        for k in range(4):
            DT[i, :, 256 * k:256 * k + 256] = D[i, 256 * k:256 * k + 256, :].T
    cz.wait_recv()
    v = hv(0, me.y, zo)
    cr1 = push(v, v, hs.at[3], hr.at[3], to_r)
    cl1 = push(v, v, hs.at[4], hr.at[4], to_l)
    share(1, v, me.y, zo)
    cr0.wait_recv()
    v = hv(0, yl, zh)
    fr = push(v, v, hs.at[5], hr.at[5], to_r)
    share(2, v, yl, zh)
    cl0.wait_recv()
    share(3, hv(0, yr, zh), yr, zh)

    oc = {}

    def osend(g, k, dev):
        oc[g, k] = push(SO.at[g, k], RO.at[g, k], os.at[g, k], orr.at[g, k], dev)

    def rows(d):
        return pl.ds(pl.multiple_of(128 * up4(me.x, d), 128), 128)

    def group(g, y):
        PG[...] = jnp.dot(DT[0], H[0, y], preferred_element_type=f32) + jnp.dot(
            DT[1], H[1, y], preferred_element_type=f32
        )
        SO[g, 0] = PG[rows(2), 0:128].astype(bf16)
        SO[g, 1] = PG[rows(2), 128:256].astype(bf16)
        osend(g, 0, xr)
        osend(g, 1, xl)
        SO[g, 3] = PG[rows(1), 128:256].astype(bf16)
        osend(g, 3, xr)
        SO[g, 4] = PG[rows(3), 0:128].astype(bf16)
        osend(g, 4, xl)
        KO[g, 0] = PG[rows(1), 0:128]
        KO[g, 1] = PG[rows(3), 128:256]
        KO[g, 2] = PG[rows(0), 0:128]
        KO[g, 3] = PG[rows(0), 128:256]

    def relay(g):
        oc[g, 0].wait_recv()
        SO[g, 2] = (KO[g, 0] + RO[g, 0].astype(f32)).astype(bf16)
        osend(g, 2, xr)
        oc[g, 1].wait_recv()
        SO[g, 5] = (KO[g, 1] + RO[g, 1].astype(f32)).astype(bf16)
        osend(g, 5, xl)

    zc = {}

    def settle(g):
        for k in (2, 3, 4, 5):
            oc[g, k].wait_recv()
        KO[g, 2] = KO[g, 2] + RO[g, 2].astype(f32) + RO[g, 4].astype(f32)
        KO[g, 3] = KO[g, 3] + RO[g, 3].astype(f32) + RO[g, 5].astype(f32)
        SZ[g, 0] = KO[g, 2].astype(bf16)
        SZ[g, 1] = KO[g, 3].astype(bf16)
        for d in (1, 2, 3):
            z = up4(me.zl, d)
            part = pl.ds(pl.multiple_of(32 * z, 32), 32)
            zc[g, d] = push(
                SZ.at[g, pl.ds(0, 2), part], RZ.at[g, d - 1], zs.at[g, d - 1], zr.at[g, d - 1], me.tid(zl=z)
            )

    def close(g, y):
        mine = pl.ds(pl.multiple_of(32 * me.zl, 32), 32)
        for d in (1, 2, 3):
            zc[g, d].wait_recv()
        for b in range(2):
            tot = KO[g, 2 + b, mine, :]
            for d in range(3):
                tot = tot + RZ[g, d, b].astype(f32)
            outt[:, pl.ds(pl.multiple_of(256 * y + 128 * b, 128), 128)] = tot

    cc[0].wait_recv()
    cc[1].wait_recv()
    group(0, me.y)
    cl1.wait_recv()
    v = hv(0, yr, zo)
    fl = push(v, v, hs.at[6], hr.at[6], to_l)
    share(4, v, yr, zo)
    cr1.wait_recv()
    share(5, hv(0, yl, zo), yl, zo)
    cc[3].wait_recv()
    cc[4].wait_recv()
    group(1, yr)
    relay(0)
    cc[2].wait_recv()
    cc[5].wait_recv()
    group(2, yl)
    relay(1)
    fr.wait_recv()
    share(6, hv(0, yf, zh), yf, zh)
    settle(0)
    fl.wait_recv()
    share(7, hv(0, yf, zo), yf, zo)
    cc[6].wait_recv()
    cc[7].wait_recv()
    group(3, yf)
    relay(2)
    settle(1)
    relay(3)
    settle(2)
    close(0, me.y)
    settle(3)
    close(1, yr)
    close(2, yl)
    close(3, yf)
    for c in [*sent, cz, cr0, cl0, cr1, cl1, fr, fl, *oc.values(), *zc.values()]:
        c.wait_send()


def stats_kernel(outt, labs, gram, coords, wall, zall, ms,
                 zb, zg, X, XR, XS, XA, XF, GB,
                 ws, wr, ms_s, ms_r, as_, ar, xs, xr, gs, gr):
    me = Spot()
    other = 1 - me.core
    mate = me.dpid(core=other)
    chips = [(dy, dz) for dy in range(4) for dz in range(2) if dy or dz]
    chip_dev = [me.dpid(y=up4(me.y, dy), zh=lax.rem(me.zh + dz, 2)) for dy, dz in chips]
    t_dev = [{"tensor": lax.rem(me.tn + d, 16)} for d in range(1, 16)]
    greet(t_dev + chip_dev + [mate])

    out = outt[...]
    mean = jnp.sum(out, axis=1, keepdims=True) / TOKENS
    cen = out - mean
    spread = jnp.sqrt(jnp.sum(cen * cen, axis=1, keepdims=True) / TOKENS + epsilon)
    z = cen / spread
    for j in range(8):
        zb[j] = z[:, 128 * j:128 * j + 128].astype(bf16)
    slot = 4 * me.x + me.zl

    def rows32(zl, x):
        return pl.ds(pl.multiple_of(32 * (4 * x + zl), 32), 32)

    ac = []
    for d in range(1, 16):
        t = lax.rem(me.tn + d, 16)
        ac.append(push(zb.at[t // 2], zg.at[rows32(me.zl, me.x)], as_.at[d - 1], ar.at[d - 1], t_dev[d - 1]))
    zg[rows32(me.zl, me.x), :] = zb[me.tn // 2]

    cls = lax.broadcasted_iota(jnp.int32, (NCLS, 128), 0)
    c1 = cen.astype(bf16)
    r1 = cen - c1.astype(f32)
    c2 = r1.astype(bf16)
    c3 = (r1 - c2.astype(f32)).astype(bf16)
    acc = jnp.zeros((32, NCLS), f32)
    for j in range(8):
        row = labs[2 * j, 0:1, :] + labs[2 * j + 1, 0:1, :]
        hot = (cls == row).astype(f32).astype(bf16)
        cols = slice(128 * j, 128 * j + 128)
        acc = acc + nt(c1[:, cols], hot) + nt(c2[:, cols], hot) + nt(c3[:, cols], hot)
    wall[rows32(me.zl, me.x), :] = (acc / TOKENS / spread).astype(bf16)
    lane = lax.broadcasted_iota(jnp.int32, (32, 128), 1)
    ms[rows32(me.zl, me.x), :] = jnp.where(lane < 64, mean, spread)

    def wv(zl, x):
        return wall.at[rows32(zl, x)]

    def mv(zl, x):
        return ms.at[rows32(zl, x)]

    sent = gather_tensor(
        me, [(wv(me.zl, me.x), wv, ws, wr), (mv(me.zl, me.x), mv, ms_s, ms_r)]
    )
    for c in ac:
        c.wait_recv()
    sent += ac
    zz = zg[...].astype(f32)
    zz = jnp.where(lax.rem(me.tn, 2) == 1, pltpu.roll(zz, 64, 1), zz)
    zall[...] = zz.astype(bf16)
    wt = wall[...].T
    G = jnp.dot(wt, wall[...], preferred_element_type=f32)
    C = jnp.dot(wt, zall[...], preferred_element_type=f32)
    gram[...] = G
    lane = lax.broadcasted_iota(jnp.int32, (128, 128), 1)
    X[0:128, :] = jnp.where(lane < 64, C[:128], pltpu.roll(C[128:], 64, 1))
    mine = pl.ds(pl.multiple_of(16 * me.tn, 16), 16)
    X[128:144, :] = gram[mine, 0:128]
    X[144:160, :] = gram[mine, 128:256]
    half = lambda c: pl.ds(pl.multiple_of(80 * c, 8), 80)
    c0 = push(X.at[half(other)], XR, xs.at[0], xr.at[0], mate)
    c0.wait_recv()
    chip = me.y * 2 + me.zh
    XS[...] = X[half(me.core), :] + XR[...]
    XA[chip] = XS[...]
    xc = []
    for k, dev in enumerate(chip_dev):
        xc.append(push(XS, XA.at[chip], xs.at[1 + k], xr.at[1 + k], dev))
    for c in xc:
        c.wait_recv()
    tot = XA[0]
    for k in range(1, 8):
        tot = tot + XA[k]
    XF[half(me.core), :] = tot
    c1x = push(XF.at[half(me.core)], XF.at[half(me.core)], xs.at[8], xr.at[8], mate)
    c1x.wait_recv()
    GB[me.tn] = XF[128:160, :]

    def gv(zl, x):
        return GB.at[4 * zl + x]

    sent += gather_tensor(me, [(gv(me.zl, me.x), gv, gs, gr)])
    for t in range(16):
        gram[16 * t:16 * t + 16, 0:128] = GB[t, 0:16, :]
        gram[16 * t:16 * t + 16, 128:256] = GB[t, 16:32, :]
    coords[0:128, :] = XF[0:128, :]
    coords[128:256, :] = pltpu.roll(XF[0:128, :], 64, 1)
    for c in [*sent, c0, *xc, c1x]:
        c.wait_send()


def params(cid):
    return pltpu.CompilerParams(collective_id=cid, has_side_effects=True, vmem_limit_bytes=56 * 2**20)


DMA = pltpu.SemaphoreType.DMA
V = pltpu.VMEM
S = jax.ShapeDtypeStruct


def shards(tokens, gate_weight, up_weight, down_weight, labels):
    tn = lax.axis_index("tensor")
    twice = jnp.concatenate([labels, labels])[None, :]
    keep = (jnp.arange(128) // 64)[None, :] == tn % 2
    lab = jnp.broadcast_to(jnp.where(keep, twice, 0), (8, 128))
    nq = len(CHUNKS)
    h, labs = pl.pallas_call(
        hidden_kernel,
        out_shape=(S((UNITS, 128), bf16), S((16, 8, 128), jnp.int32)),
        in_specs=[VM, VM, ANY, ANY],
        out_specs=(VM, VM),
        scratch_shapes=[
            V((1024, 512), bf16), V((1024, 512), bf16), V((2, 2, UNITS, 512), bf16),
            V((6, 2 * UNITS, 128), bf16), V((6, 2 * UNITS, 128), bf16), V((2, 2 * UNITS, 128), f32),
            V((2 * UNITS, 256), f32), V((2 * UNITS, 128), bf16), V((2 * UNITS, 128), bf16),
            DMA((16,)), DMA((16,)), DMA((16,)), DMA((16,)), DMA((2,)), DMA((2,)), DMA((2,)),
            DMA((4,)), DMA((4,)), DMA((6, nq)), DMA((6, nq)), DMA((nq,)), DMA((nq,)),
        ],
        compiler_params=params(0),
        name="gate_up_hidden",
    )(tokens, lab, gate_weight.T, up_weight.T)
    outt = pl.pallas_call(
        down_kernel,
        out_shape=S((32, 1024), f32),
        in_specs=[VM, ANY],
        out_specs=VM,
        scratch_shapes=[
            V((2, 1024, 512), bf16), V((2, 512, 1024), bf16), V((2, 4, 1024, 256), bf16),
            V((512, 256), f32), V((4, 4, 128, 128), f32), V((4, 6, 128, 128), bf16),
            V((4, 6, 128, 128), bf16), V((4, 2, 128, 128), bf16), V((4, 3, 2, 32, 128), bf16),
            DMA((2,)), DMA((7,)), DMA((7,)), DMA((8,)), DMA((8,)),
            DMA((4, 6)), DMA((4, 6)), DMA((4, 3)), DMA((4, 3)),
        ],
        compiler_params=params(1),
        name="down_scatter",
    )(h, down_weight)
    gram_mat, coords, wall, zall, ms = pl.pallas_call(
        stats_kernel,
        out_shape=(S((256, 256), f32), S((256, 128), f32), S((512, 256), bf16), S((512, 128), bf16), S((512, 128), f32)),
        in_specs=[VM, VM],
        out_specs=(VM, VM, VM, VM, VM),
        scratch_shapes=[
            V((8, 32, 128), bf16), V((512, 128), bf16), V((160, 128), f32), V((80, 128), f32),
            V((80, 128), f32), V((8, 80, 128), f32), V((160, 128), f32), V((16, 32, 128), f32),
            DMA((16,)), DMA((16,)), DMA((16,)), DMA((16,)), DMA((15,)), DMA((15,)),
            DMA((9,)), DMA((9,)), DMA((16,)), DMA((16,)),
        ],
        compiler_params=params(2),
        name="stats_gram",
    )(outt, labs)
    ridge_term = ridge_share * jnp.trace(gram_mat) / NCLS
    factor = jnp.linalg.cholesky(gram_mat + ridge_term * jnp.eye(NCLS, dtype=f32))
    solved = jax.scipy.linalg.cho_solve((factor, True), coords[:, :64])
    fix = jnp.dot(wall, solved.astype(bf16), preferred_element_type=f32)
    erased = ms[:, 0:1] + ms[:, 64:65] * (zall[:, :64].astype(f32) - fix)
    return erased.T.astype(bf16)


def solution(mesh):
    return jax.shard_map(
        shards,
        mesh=mesh,
        in_specs=(
            P("tensor", "dp"),
            P("dp", "tensor"),
            P("dp", "tensor"),
            P("tensor", "dp"),
            P("tensor"),
        ),
        out_specs=P("tensor", "dp"),
        check_vma=False,
    )
```

```python
import functools

import jax
import jax.numpy as jnp
from jax import lax
from jax.experimental import pallas as pl
from jax.experimental.pallas import tpu as pltpu
from jax.sharding import PartitionSpec as P

MESH = pl.DeviceIdType.MESH
NCLS = 256
TOKENS = 1024
UNITS = 928
SHIFT = 920
CHUNKS = (240, 240, 224, 224)
epsilon = 1e-05
ridge_share = 0.5
f32 = jnp.float32
bf16 = jnp.bfloat16
VM = pl.BlockSpec(memory_space=pltpu.VMEM)
ANY = pl.BlockSpec(memory_space=pl.ANY)


class Spot:
    def __init__(self):
        dp, tn = lax.axis_index("dp"), lax.axis_index("tensor")
        self.dp, self.tn = dp, tn
        self.core = lax.rem(dp, 2)
        self.zh = lax.rem(dp // 2, 2)
        self.y = dp // 4
        self.x = lax.rem(tn, 4)
        self.zl = tn // 4

    def dpid(self, y=None, zh=None, core=None):
        y = self.y if y is None else y
        zh = self.zh if zh is None else zh
        core = self.core if core is None else core
        return {"dp": y * 4 + zh * 2 + core}

    def tid(self, zl=None, x=None):
        zl = self.zl if zl is None else zl
        x = self.x if x is None else x
        return {"tensor": zl * 4 + x}


def up4(v, d):
    return lax.rem(v + d, 4)


def greet(peers):
    barrier = pltpu.get_barrier_semaphore()
    for peer in peers:
        pl.semaphore_signal(barrier, inc=1, device_id=peer, device_id_type=MESH)
    pl.semaphore_wait(barrier, len(peers))


def push(src, dst, ssem, rsem, dev):
    copy = pltpu.make_async_remote_copy(
        src_ref=src, dst_ref=dst, send_sem=ssem, recv_sem=rsem, device_id=dev, device_id_type=MESH
    )
    copy.start()
    return copy


def gather_tensor(me, parts):
    copies = []
    zc, rc, lc, fc = {}, {}, {}, {}
    right, left = up4(me.x, 1), up4(me.x, 3)
    for i, (own, block, ss, rs) in enumerate(parts):
        for d in (1, 2, 3):
            zc[i, d] = push(own, block(me.zl, me.x), ss.at[d], rs.at[d], me.tid(zl=up4(me.zl, d)))
    for d in range(4):
        z = up4(me.zl, 4 - d)
        for i, (own, block, ss, rs) in enumerate(parts):
            src = own
            if d:
                zc[i, d].wait_recv()
                src = block(z, me.x)
            rc[i, d] = push(src, block(z, me.x), ss.at[4 + d], rs.at[4 + d], me.tid(x=right))
            lc[i, d] = push(src, block(z, me.x), ss.at[8 + d], rs.at[8 + d], me.tid(x=left))
    for d in range(4):
        z = up4(me.zl, 4 - d)
        for i, (own, block, ss, rs) in enumerate(parts):
            rc[i, d].wait_recv()
            lc[i, d].wait_recv()
            if d < 2:
                v = block(z, left)
                fc[i, d] = push(v, v, ss.at[12 + d], rs.at[12 + d], me.tid(x=right))
            else:
                v = block(z, right)
                fc[i, d] = push(v, v, ss.at[12 + d], rs.at[12 + d], me.tid(x=left))
    for c in fc.values():
        c.wait_recv()
    return [*zc.values(), *rc.values(), *lc.values(), *fc.values()]


def tensor_peers(me):
    peers = [me.tid(zl=up4(me.zl, d)) for d in (1, 2, 3)]
    return peers + [me.tid(x=up4(me.x, 1)), me.tid(x=up4(me.x, 3))]


def nt(a, b):
    return lax.dot_general(a, b, (((1,), (1,)), ((), ())), preferred_element_type=f32)


def hidden_kernel(tok, lab, wg, wu, h, labs, T, Tp, W, S, R, K2, PO, SZ, RZ,
                  ts, tr, ls, lr, ws, wr, wl, cs, cr, rs, rr, zs, zr):
    me = Spot()
    other = 1 - me.core
    own_rows = pl.ds(pl.multiple_of(SHIFT * me.core, 8), UNITS)
    far_rows = pl.ds(pl.multiple_of(SHIFT * other, 8), UNITS)
    local = []
    for i, w in enumerate((wg, wu)):
        c = pltpu.make_async_copy(w.at[own_rows], W.at[0, i], wl.at[i])
        c.start()
        local.append(c)
    yr, yl = up4(me.y, 1), up4(me.y, 3)
    to_r, to_l = me.dpid(y=yr), me.dpid(y=yl)
    mate = me.dpid(core=other)
    greet(tensor_peers(me) + [to_r, to_l, me.dpid(zh=1 - me.zh), mate])
    sent = []
    wx = []
    for i, w in enumerate((wg, wu)):
        wx.append(push(w.at[far_rows], W.at[1, i], ws.at[i], wr.at[i], mate))

    def tblock(zl, x):
        return T.at[pl.ds(pl.multiple_of(64 * (4 * zl + x), 64), 64)]

    def lblock(zl, x):
        return labs.at[4 * zl + x]

    T[pl.ds(pl.multiple_of(64 * me.tn, 64), 64), :] = tok[...]
    labs[me.tn] = lab[...]
    sent += gather_tensor(me, [(tok, tblock, ts, tr), (lab, lblock, ls, lr)])
    order = (2, 1, 3, 0)
    tx = []
    for k, d in enumerate(order):
        rows = pl.ds(pl.multiple_of(256 * up4(me.y, d), 256), 256)
        tx.append(push(T.at[rows], Tp.at[rows], cs.at[k], cr.at[k], mate))
    for c in local:
        c.wait()
    for c in wx:
        c.wait_recv()
    for c in tx:
        c.wait_recv()
    sent += wx + tx

    starts = [sum(CHUNKS[:q]) for q in range(len(CHUNKS))]

    def mult(i, q, d):
        a, n = starts[q], CHUNKS[q]
        rows = pl.ds(pl.multiple_of(256 * up4(me.y, d), 256), 256)
        return nt(W[0, i, a:a + n, :], T[rows, :]) + nt(W[1, i, a:a + n, :], Tp[rows, :])

    cps = {}

    def send(k, q, dev):
        rows = pl.ds(2 * starts[q], 2 * CHUNKS[q])
        cps[k, q] = push(S.at[k, rows], R.at[k, rows], rs.at[k, q], rr.at[k, q], dev)

    def first(q):
        a, n = starts[q], CHUNKS[q]
        for i in range(2):
            o = 2 * a + i * n
            p = mult(i, q, 2)
            S[0, o:o + n, :] = p[:, :128].astype(bf16)
            S[1, o:o + n, :] = p[:, 128:].astype(bf16)
        send(0, q, to_r)
        send(1, q, to_l)
        for i in range(2):
            o = 2 * a + i * n
            p = mult(i, q, 1)
            K2[0, o:o + n, :] = p[:, :128]
            S[3, o:o + n, :] = p[:, 128:].astype(bf16)
        send(3, q, to_r)
        for i in range(2):
            o = 2 * a + i * n
            p = mult(i, q, 3)
            K2[1, o:o + n, :] = p[:, 128:]
            S[4, o:o + n, :] = p[:, :128].astype(bf16)
        send(4, q, to_l)
        for i in range(2):
            o = 2 * a + i * n
            PO[o:o + n, :] = mult(i, q, 0)

    def second(q):
        o, n = 2 * starts[q], 2 * CHUNKS[q]
        cps[0, q].wait_recv()
        S[2, o:o + n, :] = (K2[0, o:o + n, :] + R[0, o:o + n, :].astype(f32)).astype(bf16)
        send(2, q, to_r)
        cps[1, q].wait_recv()
        S[5, o:o + n, :] = (K2[1, o:o + n, :] + R[1, o:o + n, :].astype(f32)).astype(bf16)
        send(5, q, to_l)

    zc = {}

    def third(q):
        o, n = 2 * starts[q], 2 * CHUNKS[q]
        for k in (2, 3, 4, 5):
            cps[k, q].wait_recv()
        a = PO[o:o + n, :128] + R[2, o:o + n, :].astype(f32) + R[4, o:o + n, :].astype(f32)
        b = PO[o:o + n, 128:] + R[3, o:o + n, :].astype(f32) + R[5, o:o + n, :].astype(f32)
        low = me.zh == 0
        SZ[o:o + n, :] = jnp.where(low, b, a).astype(bf16)
        PO[o:o + n, :128] = jnp.where(low, a, b)
        rows = pl.ds(o, n)
        zc[q] = push(SZ.at[rows], RZ.at[rows], zs.at[q], zr.at[q], me.dpid(zh=1 - me.zh))

    def last(q):
        a, n = starts[q], CHUNKS[q]
        o = 2 * a
        zc[q].wait_recv()
        tot = PO[o:o + 2 * n, :128] + RZ[o:o + 2 * n, :].astype(f32)
        g, u = tot[:n], tot[n:]
        h[a:a + n, :] = (g / (1.0 + jnp.exp(-g)) * u).astype(bf16)

    nq = len(CHUNKS)
    for i in range(nq + 2):
        if i < nq:
            first(i)
        if 1 <= i <= nq:
            second(i - 1)
        if i >= 2:
            third(i - 2)
    for q in range(nq):
        last(q)
    for c in [*sent, *cps.values(), *zc.values()]:
        c.wait_send()


def down_kernel(h, down, outt, D, DT, H, PG, KO, SO, RO, SZ, RZ,
                dl, hs, hr, cs, cr, os, orr, zs, zr):
    me = Spot()
    other = 1 - me.core
    loads = []
    for i, c in enumerate((me.core, other)):
        cp = pltpu.make_async_copy(
            down.at[pl.ds(pl.multiple_of(SHIFT * c, 8), UNITS)], D.at[i, pl.ds(0, UNITS)], dl.at[i]
        )
        cp.start()
        loads.append(cp)
    yr, yl, yf = up4(me.y, 1), up4(me.y, 3), up4(me.y, 2)
    to_r, to_l = me.dpid(y=yr), me.dpid(y=yl)
    mate = me.dpid(core=other)
    across = me.dpid(zh=1 - me.zh)
    xr, xl = me.tid(x=up4(me.x, 1)), me.tid(x=up4(me.x, 3))
    greet(tensor_peers(me) + [to_r, to_l, across, mate])

    def hv(i, y, zh):
        return H.at[i, y, pl.ds(0, UNITS), pl.ds(pl.multiple_of(128 * zh, 128), 128)]

    zh, zo = me.zh, 1 - me.zh
    sent = []
    cc = {}

    def share(k, src, y, z):
        cc[k] = push(src, hv(1, y, z), cs.at[k], cr.at[k], mate)
        sent.append(cc[k])

    cz = push(h, hv(0, me.y, zh), hs.at[0], hr.at[0], across)
    cr0 = push(h, hv(0, me.y, zh), hs.at[1], hr.at[1], to_r)
    cl0 = push(h, hv(0, me.y, zh), hs.at[2], hr.at[2], to_l)
    share(0, h, me.y, zh)
    H[0, me.y, 0:UNITS, pl.ds(pl.multiple_of(128 * zh, 128), 128)] = h[...]
    H[:, :, UNITS:, :] = jnp.zeros((2, 4, 1024 - UNITS, 256), bf16)
    for i in range(2):
        loads[i].wait()
        D[i, UNITS:, :] = jnp.zeros((1024 - UNITS, 512), bf16)
        dup = (me.core if i == 0 else other) == 1
        head = D[i, 0:16, :].astype(f32)
        row = lax.broadcasted_iota(jnp.int32, head.shape, 0)
        D[i, 0:16, :] = jnp.where(jnp.logical_and(dup, row < 8), 0.0, head).astype(bf16)
        for k in range(4):
            DT[i, :, 256 * k:256 * k + 256] = D[i, 256 * k:256 * k + 256, :].T
    cz.wait_recv()
    v = hv(0, me.y, zo)
    cr1 = push(v, v, hs.at[3], hr.at[3], to_r)
    cl1 = push(v, v, hs.at[4], hr.at[4], to_l)
    share(1, v, me.y, zo)
    cr0.wait_recv()
    v = hv(0, yl, zh)
    fr = push(v, v, hs.at[5], hr.at[5], to_r)
    share(2, v, yl, zh)
    cl0.wait_recv()
    share(3, hv(0, yr, zh), yr, zh)

    oc = {}

    def osend(g, k, dev):
        oc[g, k] = push(SO.at[g, k], RO.at[g, k], os.at[g, k], orr.at[g, k], dev)

    def rows(d):
        return pl.ds(pl.multiple_of(128 * up4(me.x, d), 128), 128)

    def group(g, y):
        PG[...] = jnp.dot(DT[0], H[0, y], preferred_element_type=f32) + jnp.dot(
            DT[1], H[1, y], preferred_element_type=f32
        )
        SO[g, 0] = PG[rows(2), 0:128].astype(bf16)
        SO[g, 1] = PG[rows(2), 128:256].astype(bf16)
        osend(g, 0, xr)
        osend(g, 1, xl)
        SO[g, 3] = PG[rows(1), 128:256].astype(bf16)
        osend(g, 3, xr)
        SO[g, 4] = PG[rows(3), 0:128].astype(bf16)
        osend(g, 4, xl)
        KO[g, 0] = PG[rows(1), 0:128]
        KO[g, 1] = PG[rows(3), 128:256]
        KO[g, 2] = PG[rows(0), 0:128]
        KO[g, 3] = PG[rows(0), 128:256]

    def relay(g):
        oc[g, 0].wait_recv()
        SO[g, 2] = (KO[g, 0] + RO[g, 0].astype(f32)).astype(bf16)
        osend(g, 2, xr)
        oc[g, 1].wait_recv()
        SO[g, 5] = (KO[g, 1] + RO[g, 1].astype(f32)).astype(bf16)
        osend(g, 5, xl)

    zc = {}

    def settle(g):
        for k in (2, 3, 4, 5):
            oc[g, k].wait_recv()
        KO[g, 2] = KO[g, 2] + RO[g, 2].astype(f32) + RO[g, 4].astype(f32)
        KO[g, 3] = KO[g, 3] + RO[g, 3].astype(f32) + RO[g, 5].astype(f32)
        SZ[g, 0] = KO[g, 2].astype(bf16)
        SZ[g, 1] = KO[g, 3].astype(bf16)
        for d in (1, 2, 3):
            z = up4(me.zl, d)
            part = pl.ds(pl.multiple_of(32 * z, 32), 32)
            zc[g, d] = push(
                SZ.at[g, pl.ds(0, 2), part], RZ.at[g, d - 1], zs.at[g, d - 1], zr.at[g, d - 1], me.tid(zl=z)
            )

    def close(g, y):
        mine = pl.ds(pl.multiple_of(32 * me.zl, 32), 32)
        for d in (1, 2, 3):
            zc[g, d].wait_recv()
        for b in range(2):
            tot = KO[g, 2 + b, mine, :]
            for d in range(3):
                tot = tot + RZ[g, d, b].astype(f32)
            outt[:, pl.ds(pl.multiple_of(256 * y + 128 * b, 128), 128)] = tot

    cc[0].wait_recv()
    cc[1].wait_recv()
    group(0, me.y)
    cl1.wait_recv()
    v = hv(0, yr, zo)
    fl = push(v, v, hs.at[6], hr.at[6], to_l)
    share(4, v, yr, zo)
    cr1.wait_recv()
    share(5, hv(0, yl, zo), yl, zo)
    cc[3].wait_recv()
    cc[4].wait_recv()
    group(1, yr)
    relay(0)
    cc[2].wait_recv()
    cc[5].wait_recv()
    group(2, yl)
    relay(1)
    fr.wait_recv()
    share(6, hv(0, yf, zh), yf, zh)
    settle(0)
    fl.wait_recv()
    share(7, hv(0, yf, zo), yf, zo)
    cc[6].wait_recv()
    cc[7].wait_recv()
    group(3, yf)
    relay(2)
    settle(1)
    relay(3)
    settle(2)
    close(0, me.y)
    settle(3)
    close(1, yr)
    close(2, yl)
    close(3, yf)
    for c in [*sent, cz, cr0, cl0, cr1, cl1, fr, fl, *oc.values(), *zc.values()]:
        c.wait_send()


def scales():
    low, out = 1.0 / 513.0, []
    for _ in range(8):
        out.append(2.0 / (1.0 + low))
        low = 4.0 * low / (1.0 + low) ** 2
    return out


def solve(FY, gram, coords):
    sc = scales()
    eye = lax.broadcasted_iota(jnp.int32, (NCLS, NCLS), 0) == lax.broadcasted_iota(jnp.int32, (NCLS, NCLS), 1)
    G = gram[...]
    diag = jnp.where(eye, G, 0.0)
    trace = jnp.sum(jnp.sum(diag, axis=1, keepdims=True), axis=0, keepdims=True)
    ridge = ridge_share * trace / NCLS
    inv = 1.0 / (513.0 * ridge)
    FY[:, :NCLS] = jnp.where(eye, 1.0 - sc[0] / 513.0, 0.0) - (sc[0] * inv) * G
    FY[:, NCLS:] = coords[...]

    def pick(k, vals):
        out = jnp.float32(vals[0])
        for i in range(1, len(vals)):
            out = jnp.where(k == i, jnp.float32(vals[i]), out)
        return out

    def step(k, carry):
        now, nxt = pick(k, sc[:7]), pick(k, sc[1:])
        both = jnp.dot(FY[:, :NCLS], FY[...], precision=lax.Precision.HIGHEST, preferred_element_type=f32)
        FY[:, NCLS:] = now * (FY[:, NCLS:] + both[:, NCLS:])
        FY[:, :NCLS] = nxt * both[:, :NCLS] + jnp.where(eye, 1.0 - nxt, 0.0)
        return carry

    lax.fori_loop(0, 7, step, 0)
    Y = FY[:, NCLS:]
    last = jnp.dot(FY[:, :NCLS], Y, precision=lax.Precision.HIGHEST, preferred_element_type=f32)
    return (sc[7] * inv) * (Y + last)


def stats_kernel(outt, labs, erased, gram, coords, wall, ms, FY,
                 zb, zg, X, XR, XS, XA, XF, GB,
                 ws, wr, ms_s, ms_r, as_, ar, xs, xr, gs, gr):
    me = Spot()
    other = 1 - me.core
    mate = me.dpid(core=other)
    chips = [(dy, dz) for dy in range(4) for dz in range(2) if dy or dz]
    chip_dev = [me.dpid(y=up4(me.y, dy), zh=lax.rem(me.zh + dz, 2)) for dy, dz in chips]
    t_dev = [{"tensor": lax.rem(me.tn + d, 16)} for d in range(1, 16)]
    greet(t_dev + chip_dev + [mate])

    out = outt[...]
    mean = jnp.sum(out, axis=1, keepdims=True) / TOKENS
    cen = out - mean
    spread = jnp.sqrt(jnp.sum(cen * cen, axis=1, keepdims=True) / TOKENS + epsilon)
    z = cen / spread
    for j in range(8):
        zb[j] = z[:, 128 * j:128 * j + 128].astype(bf16)
    slot = 4 * me.x + me.zl

    def rows32(zl, x):
        return pl.ds(pl.multiple_of(32 * (4 * x + zl), 32), 32)

    ac = []
    for d in range(1, 16):
        t = lax.rem(me.tn + d, 16)
        ac.append(push(zb.at[t // 2], zg.at[rows32(me.zl, me.x)], as_.at[d - 1], ar.at[d - 1], t_dev[d - 1]))
    zg[rows32(me.zl, me.x), :] = zb[me.tn // 2]

    cls = lax.broadcasted_iota(jnp.int32, (NCLS, 128), 0)
    c1 = cen.astype(bf16)
    r1 = cen - c1.astype(f32)
    c2 = r1.astype(bf16)
    c3 = (r1 - c2.astype(f32)).astype(bf16)
    acc = jnp.zeros((32, NCLS), f32)
    for j in range(8):
        row = labs[2 * j, 0:1, :] + labs[2 * j + 1, 0:1, :]
        hot = (cls == row).astype(f32).astype(bf16)
        cols = slice(128 * j, 128 * j + 128)
        acc = acc + nt(c1[:, cols], hot) + nt(c2[:, cols], hot) + nt(c3[:, cols], hot)
    wall[rows32(me.zl, me.x), :] = (acc / TOKENS / spread).astype(bf16)
    lane = lax.broadcasted_iota(jnp.int32, (32, 128), 1)
    ms[rows32(me.zl, me.x), :] = jnp.where(lane < 64, mean, spread)

    def wv(zl, x):
        return wall.at[rows32(zl, x)]

    def mv(zl, x):
        return ms.at[rows32(zl, x)]

    sent = gather_tensor(
        me, [(wv(me.zl, me.x), wv, ws, wr), (mv(me.zl, me.x), mv, ms_s, ms_r)]
    )
    for c in ac:
        c.wait_recv()
    sent += ac
    zz = zg[...].astype(f32)
    zz = jnp.where(lax.rem(me.tn, 2) == 1, pltpu.roll(zz, 64, 1), zz)
    zall = zz.astype(bf16)
    wt = wall[...].T
    G = jnp.dot(wt, wall[...], preferred_element_type=f32)
    C = jnp.dot(wt, zall, preferred_element_type=f32)
    gram[...] = G
    lane = lax.broadcasted_iota(jnp.int32, (128, 128), 1)
    X[0:128, :] = jnp.where(lane < 64, C[:128], pltpu.roll(C[128:], 64, 1))
    mine = pl.ds(pl.multiple_of(16 * me.tn, 16), 16)
    X[128:144, :] = gram[mine, 0:128]
    X[144:160, :] = gram[mine, 128:256]
    half = lambda c: pl.ds(pl.multiple_of(80 * c, 8), 80)
    c0 = push(X.at[half(other)], XR, xs.at[0], xr.at[0], mate)
    c0.wait_recv()
    chip = me.y * 2 + me.zh
    XS[...] = X[half(me.core), :] + XR[...]
    XA[chip] = XS[...]
    xc = []
    for k, dev in enumerate(chip_dev):
        xc.append(push(XS, XA.at[chip], xs.at[1 + k], xr.at[1 + k], dev))
    for c in xc:
        c.wait_recv()
    tot = XA[0]
    for k in range(1, 8):
        tot = tot + XA[k]
    XF[half(me.core), :] = tot
    c1x = push(XF.at[half(me.core)], XF.at[half(me.core)], xs.at[8], xr.at[8], mate)
    c1x.wait_recv()
    GB[me.tn] = XF[128:160, :]

    def gv(zl, x):
        return GB.at[4 * zl + x]

    sent += gather_tensor(me, [(gv(me.zl, me.x), gv, gs, gr)])
    for t in range(16):
        gram[16 * t:16 * t + 16, 0:128] = GB[t, 0:16, :]
        gram[16 * t:16 * t + 16, 128:256] = GB[t, 16:32, :]
    coords[0:128, :] = XF[0:128, :]
    coords[128:256, :] = pltpu.roll(XF[0:128, :], 64, 1)
    solved = solve(FY, gram, coords)
    fix = jnp.dot(wall[...], solved.astype(bf16), preferred_element_type=f32)
    done = ms[:, 0:1] + ms[:, 64:65] * (zz - fix)
    erased[...] = done.T[:64].astype(bf16)
    for c in [*sent, c0, *xc, c1x]:
        c.wait_send()


def params(cid):
    return pltpu.CompilerParams(collective_id=cid, has_side_effects=True, vmem_limit_bytes=56 * 2**20)


DMA = pltpu.SemaphoreType.DMA
V = pltpu.VMEM
S = jax.ShapeDtypeStruct


def shards(tokens, gate_weight, up_weight, down_weight, labels):
    tn = lax.axis_index("tensor")
    twice = jnp.concatenate([labels, labels])[None, :]
    keep = (jnp.arange(128) // 64)[None, :] == tn % 2
    lab = jnp.broadcast_to(jnp.where(keep, twice, 0), (8, 128))
    nq = len(CHUNKS)
    h, labs = pl.pallas_call(
        hidden_kernel,
        out_shape=(S((UNITS, 128), bf16), S((16, 8, 128), jnp.int32)),
        in_specs=[VM, VM, ANY, ANY],
        out_specs=(VM, VM),
        scratch_shapes=[
            V((1024, 512), bf16), V((1024, 512), bf16), V((2, 2, UNITS, 512), bf16),
            V((6, 2 * UNITS, 128), bf16), V((6, 2 * UNITS, 128), bf16), V((2, 2 * UNITS, 128), f32),
            V((2 * UNITS, 256), f32), V((2 * UNITS, 128), bf16), V((2 * UNITS, 128), bf16),
            DMA((16,)), DMA((16,)), DMA((16,)), DMA((16,)), DMA((2,)), DMA((2,)), DMA((2,)),
            DMA((4,)), DMA((4,)), DMA((6, nq)), DMA((6, nq)), DMA((nq,)), DMA((nq,)),
        ],
        compiler_params=params(0),
        name="gate_up_hidden",
    )(tokens, lab, gate_weight.T, up_weight.T)
    outt = pl.pallas_call(
        down_kernel,
        out_shape=S((32, 1024), f32),
        in_specs=[VM, ANY],
        out_specs=VM,
        scratch_shapes=[
            V((2, 1024, 512), bf16), V((2, 512, 1024), bf16), V((2, 4, 1024, 256), bf16),
            V((512, 256), f32), V((4, 4, 128, 128), f32), V((4, 6, 128, 128), bf16),
            V((4, 6, 128, 128), bf16), V((4, 2, 128, 128), bf16), V((4, 3, 2, 32, 128), bf16),
            DMA((2,)), DMA((7,)), DMA((7,)), DMA((8,)), DMA((8,)),
            DMA((4, 6)), DMA((4, 6)), DMA((4, 3)), DMA((4, 3)),
        ],
        compiler_params=params(1),
        name="down_scatter",
    )(h, down_weight)
    return pl.pallas_call(
        stats_kernel,
        out_shape=S((64, 512), bf16),
        in_specs=[VM, VM],
        out_specs=VM,
        scratch_shapes=[
            V((256, 256), f32), V((256, 128), f32), V((512, 256), bf16), V((512, 128), f32), V((256, 384), f32),
            V((8, 32, 128), bf16), V((512, 128), bf16), V((160, 128), f32), V((80, 128), f32),
            V((80, 128), f32), V((8, 80, 128), f32), V((160, 128), f32), V((16, 32, 128), f32),
            DMA((16,)), DMA((16,)), DMA((16,)), DMA((16,)), DMA((15,)), DMA((15,)),
            DMA((9,)), DMA((9,)), DMA((16,)), DMA((16,)),
        ],
        compiler_params=params(2),
        name="stats_solve_erase",
    )(outt, labs)


def solution(mesh):
    return jax.shard_map(
        shards,
        mesh=mesh,
        in_specs=(
            P("tensor", "dp"),
            P("dp", "tensor"),
            P("dp", "tensor"),
            P("tensor", "dp"),
            P("tensor"),
        ),
        out_specs=P("tensor", "dp"),
        check_vma=False,
    )
```

```python
import functools

import jax
import jax.numpy as jnp
from jax import lax
from jax.experimental import pallas as pl
from jax.experimental.pallas import tpu as pltpu
from jax.sharding import PartitionSpec as P

MESH = pl.DeviceIdType.MESH
NCLS = 256
TOKENS = 1024
UNITS = 928
SHIFT = 920
CHUNKS = (240, 240, 224, 224)
epsilon = 1e-05
ridge_share = 0.5
f32 = jnp.float32
bf16 = jnp.bfloat16
VM = pl.BlockSpec(memory_space=pltpu.VMEM)
ANY = pl.BlockSpec(memory_space=pl.ANY)


class Spot:
    def __init__(self):
        dp, tn = lax.axis_index("dp"), lax.axis_index("tensor")
        self.dp, self.tn = dp, tn
        self.core = lax.rem(dp, 2)
        self.zh = lax.rem(dp // 2, 2)
        self.y = dp // 4
        self.x = lax.rem(tn, 4)
        self.zl = tn // 4

    def dpid(self, y=None, zh=None, core=None):
        y = self.y if y is None else y
        zh = self.zh if zh is None else zh
        core = self.core if core is None else core
        return {"dp": y * 4 + zh * 2 + core}

    def tid(self, zl=None, x=None):
        zl = self.zl if zl is None else zl
        x = self.x if x is None else x
        return {"tensor": zl * 4 + x}


def up4(v, d):
    return lax.rem(v + d, 4)


def greet(peers):
    barrier = pltpu.get_barrier_semaphore()
    for peer in peers:
        pl.semaphore_signal(barrier, inc=1, device_id=peer, device_id_type=MESH)
    pl.semaphore_wait(barrier, len(peers))


def push(src, dst, ssem, rsem, dev):
    copy = pltpu.make_async_remote_copy(
        src_ref=src, dst_ref=dst, send_sem=ssem, recv_sem=rsem, device_id=dev, device_id_type=MESH
    )
    copy.start()
    return copy


def gather_tensor(me, parts, done=None):
    copies = []
    zc, rc, lc, fc = {}, {}, {}, {}
    right, left = up4(me.x, 1), up4(me.x, 3)
    for i, (own, block, ss, rs) in enumerate(parts):
        for d in (1, 2, 3):
            zc[i, d] = push(own, block(me.zl, me.x), ss.at[d], rs.at[d], me.tid(zl=up4(me.zl, d)))
    for d in range(4):
        z = up4(me.zl, 4 - d)
        for i, (own, block, ss, rs) in enumerate(parts):
            src = own
            if d:
                zc[i, d].wait_recv()
                src = block(z, me.x)
            rc[i, d] = push(src, block(z, me.x), ss.at[4 + d], rs.at[4 + d], me.tid(x=right))
            lc[i, d] = push(src, block(z, me.x), ss.at[8 + d], rs.at[8 + d], me.tid(x=left))
    for d in range(4):
        z = up4(me.zl, 4 - d)
        for i, (own, block, ss, rs) in enumerate(parts):
            rc[i, d].wait_recv()
            lc[i, d].wait_recv()
            if d < 2:
                v = block(z, left)
                fc[i, d] = push(v, v, ss.at[12 + d], rs.at[12 + d], me.tid(x=right))
            else:
                v = block(z, right)
                fc[i, d] = push(v, v, ss.at[12 + d], rs.at[12 + d], me.tid(x=left))
    for d in range(4):
        for i in range(len(parts)):
            fc[i, d].wait_recv()
        if done is not None:
            done(d)
    return [*zc.values(), *rc.values(), *lc.values(), *fc.values()]


def tensor_peers(me):
    peers = [me.tid(zl=up4(me.zl, d)) for d in (1, 2, 3)]
    return peers + [me.tid(x=up4(me.x, 1)), me.tid(x=up4(me.x, 3))]


def nt(a, b):
    return lax.dot_general(a, b, (((1,), (1,)), ((), ())), preferred_element_type=f32)


def hidden_kernel(tok, lab, wg, wu, h, labs, T, Tp, W, S, R, K2, PO, SZ, RZ,
                  ts, tr, ls, lr, ws, wr, wl, cs, cr, rs, rr, zs, zr):
    me = Spot()
    other = 1 - me.core
    own_rows = pl.ds(pl.multiple_of(SHIFT * me.core, 8), UNITS)
    far_rows = pl.ds(pl.multiple_of(SHIFT * other, 8), UNITS)
    local = []
    for i, w in enumerate((wg, wu)):
        c = pltpu.make_async_copy(w.at[own_rows], W.at[0, i], wl.at[i])
        c.start()
        local.append(c)
    yr, yl = up4(me.y, 1), up4(me.y, 3)
    to_r, to_l = me.dpid(y=yr), me.dpid(y=yl)
    mate = me.dpid(core=other)
    greet(tensor_peers(me) + [to_r, to_l, me.dpid(zh=1 - me.zh), mate])
    sent = []
    wx = []
    for i, w in enumerate((wg, wu)):
        wx.append(push(w.at[far_rows], W.at[1, i], ws.at[i], wr.at[i], mate))

    def tblock(zl, x):
        return T.at[pl.ds(pl.multiple_of(64 * (4 * zl + x), 64), 64)]

    def lblock(zl, x):
        return labs.at[4 * zl + x]

    T[pl.ds(pl.multiple_of(64 * me.tn, 64), 64), :] = tok[...]
    labs[me.tn] = lab[...]
    tx = []

    def share_plane(d):
        rows = pl.ds(pl.multiple_of(256 * up4(me.zl, 4 - d), 256), 256)
        tx.append(push(T.at[rows], Tp.at[rows], cs.at[d], cr.at[d], mate))

    sent += gather_tensor(me, [(tok, tblock, ts, tr), (lab, lblock, ls, lr)], share_plane)
    for c in local:
        c.wait()
    for c in wx:
        c.wait_recv()
    sent += wx + tx

    def mate_tokens(d):
        y = up4(me.y, d)
        k = up4(me.zl, 4 - y)
        rows = pl.ds(pl.multiple_of(256 * y, 256), 256)
        pltpu.make_async_remote_copy(
            src_ref=T.at[rows], dst_ref=Tp.at[rows], send_sem=cs.at[k], recv_sem=cr.at[k],
            device_id=mate, device_id_type=MESH,
        ).wait_recv()

    starts = [sum(CHUNKS[:q]) for q in range(len(CHUNKS))]

    def mult(i, q, d):
        a, n = starts[q], CHUNKS[q]
        rows = pl.ds(pl.multiple_of(256 * up4(me.y, d), 256), 256)
        return nt(W[0, i, a:a + n, :], T[rows, :]) + nt(W[1, i, a:a + n, :], Tp[rows, :])

    cps = {}

    def send(k, q, dev):
        rows = pl.ds(2 * starts[q], 2 * CHUNKS[q])
        cps[k, q] = push(S.at[k, rows], R.at[k, rows], rs.at[k, q], rr.at[k, q], dev)

    def first(q):
        a, n = starts[q], CHUNKS[q]
        if q == 0:
            mate_tokens(2)
        for i in range(2):
            o = 2 * a + i * n
            p = mult(i, q, 2)
            S[0, o:o + n, :] = p[:, :128].astype(bf16)
            S[1, o:o + n, :] = p[:, 128:].astype(bf16)
        send(0, q, to_r)
        send(1, q, to_l)
        if q == 0:
            mate_tokens(1)
        for i in range(2):
            o = 2 * a + i * n
            p = mult(i, q, 1)
            K2[0, o:o + n, :] = p[:, :128]
            S[3, o:o + n, :] = p[:, 128:].astype(bf16)
        send(3, q, to_r)
        if q == 0:
            mate_tokens(3)
        for i in range(2):
            o = 2 * a + i * n
            p = mult(i, q, 3)
            K2[1, o:o + n, :] = p[:, 128:]
            S[4, o:o + n, :] = p[:, :128].astype(bf16)
        send(4, q, to_l)
        if q == 0:
            mate_tokens(0)
        for i in range(2):
            o = 2 * a + i * n
            PO[o:o + n, :] = mult(i, q, 0)

    def second(q):
        o, n = 2 * starts[q], 2 * CHUNKS[q]
        cps[0, q].wait_recv()
        S[2, o:o + n, :] = (K2[0, o:o + n, :] + R[0, o:o + n, :].astype(f32)).astype(bf16)
        send(2, q, to_r)
        cps[1, q].wait_recv()
        S[5, o:o + n, :] = (K2[1, o:o + n, :] + R[1, o:o + n, :].astype(f32)).astype(bf16)
        send(5, q, to_l)

    zc = {}

    def third(q):
        o, n = 2 * starts[q], 2 * CHUNKS[q]
        for k in (2, 3, 4, 5):
            cps[k, q].wait_recv()
        a = PO[o:o + n, :128] + R[2, o:o + n, :].astype(f32) + R[4, o:o + n, :].astype(f32)
        b = PO[o:o + n, 128:] + R[3, o:o + n, :].astype(f32) + R[5, o:o + n, :].astype(f32)
        low = me.zh == 0
        SZ[o:o + n, :] = jnp.where(low, b, a).astype(bf16)
        PO[o:o + n, :128] = jnp.where(low, a, b)
        rows = pl.ds(o, n)
        zc[q] = push(SZ.at[rows], RZ.at[rows], zs.at[q], zr.at[q], me.dpid(zh=1 - me.zh))

    def last(q):
        a, n = starts[q], CHUNKS[q]
        o = 2 * a
        zc[q].wait_recv()
        tot = PO[o:o + 2 * n, :128] + RZ[o:o + 2 * n, :].astype(f32)
        g, u = tot[:n], tot[n:]
        h[a:a + n, :] = (g / (1.0 + jnp.exp(-g)) * u).astype(bf16)

    nq = len(CHUNKS)
    for i in range(nq + 2):
        if i < nq:
            first(i)
        if 1 <= i <= nq:
            second(i - 1)
        if i >= 2:
            third(i - 2)
    for q in range(nq):
        last(q)
    for c in [*sent, *cps.values(), *zc.values()]:
        c.wait_send()


def down_kernel(h, down, outt, D, DT, H, PG, KO, SO, RO, SZ, RZ,
                dl, hs, hr, cs, cr, os, orr, zs, zr):
    me = Spot()
    other = 1 - me.core
    loads = []
    for i, c in enumerate((me.core, other)):
        cp = pltpu.make_async_copy(
            down.at[pl.ds(pl.multiple_of(SHIFT * c, 8), UNITS)], D.at[i, pl.ds(0, UNITS)], dl.at[i]
        )
        cp.start()
        loads.append(cp)
    yr, yl, yf = up4(me.y, 1), up4(me.y, 3), up4(me.y, 2)
    to_r, to_l = me.dpid(y=yr), me.dpid(y=yl)
    mate = me.dpid(core=other)
    across = me.dpid(zh=1 - me.zh)
    xr, xl = me.tid(x=up4(me.x, 1)), me.tid(x=up4(me.x, 3))
    greet(tensor_peers(me) + [to_r, to_l, across, mate])

    def hv(i, y, zh):
        return H.at[i, y, pl.ds(0, UNITS), pl.ds(pl.multiple_of(128 * zh, 128), 128)]

    zh, zo = me.zh, 1 - me.zh
    sent = []
    cc = {}

    def share(k, src, y, z):
        cc[k] = push(src, hv(1, y, z), cs.at[k], cr.at[k], mate)
        sent.append(cc[k])

    cz = push(h, hv(0, me.y, zh), hs.at[0], hr.at[0], across)
    cr0 = push(h, hv(0, me.y, zh), hs.at[1], hr.at[1], to_r)
    cl0 = push(h, hv(0, me.y, zh), hs.at[2], hr.at[2], to_l)
    share(0, h, me.y, zh)
    H[0, me.y, 0:UNITS, pl.ds(pl.multiple_of(128 * zh, 128), 128)] = h[...]
    H[:, :, UNITS:, :] = jnp.zeros((2, 4, 1024 - UNITS, 256), bf16)
    for i in range(2):
        loads[i].wait()
        D[i, UNITS:, :] = jnp.zeros((1024 - UNITS, 512), bf16)
        dup = (me.core if i == 0 else other) == 1
        head = D[i, 0:16, :].astype(f32)
        row = lax.broadcasted_iota(jnp.int32, head.shape, 0)
        D[i, 0:16, :] = jnp.where(jnp.logical_and(dup, row < 8), 0.0, head).astype(bf16)
        for k in range(4):
            DT[i, :, 256 * k:256 * k + 256] = D[i, 256 * k:256 * k + 256, :].T
    cz.wait_recv()
    v = hv(0, me.y, zo)
    cr1 = push(v, v, hs.at[3], hr.at[3], to_r)
    cl1 = push(v, v, hs.at[4], hr.at[4], to_l)
    share(1, v, me.y, zo)
    cr0.wait_recv()
    v = hv(0, yl, zh)
    fr = push(v, v, hs.at[5], hr.at[5], to_r)
    share(2, v, yl, zh)
    cl0.wait_recv()
    share(3, hv(0, yr, zh), yr, zh)

    oc = {}

    def osend(g, k, dev):
        oc[g, k] = push(SO.at[g, k], RO.at[g, k], os.at[g, k], orr.at[g, k], dev)

    def rows(d):
        return pl.ds(pl.multiple_of(128 * up4(me.x, d), 128), 128)

    def group(g, y):
        PG[...] = jnp.dot(DT[0], H[0, y], preferred_element_type=f32) + jnp.dot(
            DT[1], H[1, y], preferred_element_type=f32
        )
        SO[g, 0] = PG[rows(2), 0:128].astype(bf16)
        SO[g, 1] = PG[rows(2), 128:256].astype(bf16)
        osend(g, 0, xr)
        osend(g, 1, xl)
        SO[g, 3] = PG[rows(1), 128:256].astype(bf16)
        osend(g, 3, xr)
        SO[g, 4] = PG[rows(3), 0:128].astype(bf16)
        osend(g, 4, xl)
        KO[g, 0] = PG[rows(1), 0:128]
        KO[g, 1] = PG[rows(3), 128:256]
        KO[g, 2] = PG[rows(0), 0:128]
        KO[g, 3] = PG[rows(0), 128:256]

    def relay(g):
        oc[g, 0].wait_recv()
        SO[g, 2] = (KO[g, 0] + RO[g, 0].astype(f32)).astype(bf16)
        osend(g, 2, xr)
        oc[g, 1].wait_recv()
        SO[g, 5] = (KO[g, 1] + RO[g, 1].astype(f32)).astype(bf16)
        osend(g, 5, xl)

    zc = {}

    def settle(g):
        for k in (2, 3, 4, 5):
            oc[g, k].wait_recv()
        KO[g, 2] = KO[g, 2] + RO[g, 2].astype(f32) + RO[g, 4].astype(f32)
        KO[g, 3] = KO[g, 3] + RO[g, 3].astype(f32) + RO[g, 5].astype(f32)
        SZ[g, 0] = KO[g, 2].astype(bf16)
        SZ[g, 1] = KO[g, 3].astype(bf16)
        for d in (1, 2, 3):
            z = up4(me.zl, d)
            part = pl.ds(pl.multiple_of(32 * z, 32), 32)
            zc[g, d] = push(
                SZ.at[g, pl.ds(0, 2), part], RZ.at[g, d - 1], zs.at[g, d - 1], zr.at[g, d - 1], me.tid(zl=z)
            )

    def close(g, y):
        mine = pl.ds(pl.multiple_of(32 * me.zl, 32), 32)
        for d in (1, 2, 3):
            zc[g, d].wait_recv()
        for b in range(2):
            tot = KO[g, 2 + b, mine, :]
            for d in range(3):
                tot = tot + RZ[g, d, b].astype(f32)
            outt[:, pl.ds(pl.multiple_of(256 * y + 128 * b, 128), 128)] = tot

    cc[0].wait_recv()
    cc[1].wait_recv()
    group(0, me.y)
    cl1.wait_recv()
    v = hv(0, yr, zo)
    fl = push(v, v, hs.at[6], hr.at[6], to_l)
    share(4, v, yr, zo)
    cr1.wait_recv()
    share(5, hv(0, yl, zo), yl, zo)
    cc[3].wait_recv()
    cc[4].wait_recv()
    group(1, yr)
    relay(0)
    cc[2].wait_recv()
    cc[5].wait_recv()
    group(2, yl)
    relay(1)
    fr.wait_recv()
    share(6, hv(0, yf, zh), yf, zh)
    settle(0)
    fl.wait_recv()
    share(7, hv(0, yf, zo), yf, zo)
    cc[6].wait_recv()
    cc[7].wait_recv()
    group(3, yf)
    relay(2)
    settle(1)
    relay(3)
    settle(2)
    close(0, me.y)
    settle(3)
    close(1, yr)
    close(2, yl)
    close(3, yf)
    for c in [*sent, cz, cr0, cl0, cr1, cl1, fr, fl, *oc.values(), *zc.values()]:
        c.wait_send()


def scales():
    low, out = 1.0 / 513.0, []
    for _ in range(8):
        out.append(2.0 / (1.0 + low))
        low = 4.0 * low / (1.0 + low) ** 2
    return out


def solve(FY, gram, coords):
    sc = scales()
    eye = lax.broadcasted_iota(jnp.int32, (NCLS, NCLS), 0) == lax.broadcasted_iota(jnp.int32, (NCLS, NCLS), 1)
    G = gram[...]
    diag = jnp.where(eye, G, 0.0)
    trace = jnp.sum(jnp.sum(diag, axis=1, keepdims=True), axis=0, keepdims=True)
    ridge = ridge_share * trace / NCLS
    inv = 1.0 / (513.0 * ridge)
    FY[:, :NCLS] = jnp.where(eye, 1.0 - sc[0] / 513.0, 0.0) - (sc[0] * inv) * G
    FY[:, NCLS:] = coords[...]

    def pick(k, vals):
        out = jnp.float32(vals[0])
        for i in range(1, len(vals)):
            out = jnp.where(k == i, jnp.float32(vals[i]), out)
        return out

    def step(k, carry):
        now, nxt = pick(k, sc[:7]), pick(k, sc[1:])
        both = jnp.dot(FY[:, :NCLS], FY[...], precision=lax.Precision.HIGHEST, preferred_element_type=f32)
        FY[:, NCLS:] = now * (FY[:, NCLS:] + both[:, NCLS:])
        FY[:, :NCLS] = nxt * both[:, :NCLS] + jnp.where(eye, 1.0 - nxt, 0.0)
        return carry

    lax.fori_loop(0, 7, step, 0)
    Y = FY[:, NCLS:]
    last = jnp.dot(FY[:, :NCLS], Y, precision=lax.Precision.HIGHEST, preferred_element_type=f32)
    return (sc[7] * inv) * (Y + last)


def stats_kernel(outt, labs, erased, gram, coords, wall, ms, rowbuf, FY,
                 zb, zg, XG, RG, SG, ZG, AG, GB, XC, RC, SC, ZC, AC,
                 ws, wr, ms_s, ms_r, as_, ar, xs, xr, gs, gr):
    me = Spot()
    other = 1 - me.core
    mate = me.dpid(core=other)
    across = me.dpid(zh=1 - me.zh)
    y_dev = [me.dpid(y=up4(me.y, d)) for d in (1, 2, 3)]
    t_dev = [{"tensor": lax.rem(me.tn + d, 16)} for d in range(1, 16)]
    greet(t_dev + y_dev + [across, mate])

    out = outt[...]
    mean = jnp.sum(out, axis=1, keepdims=True) / TOKENS
    cen = out - mean
    spread = jnp.sqrt(jnp.sum(cen * cen, axis=1, keepdims=True) / TOKENS + epsilon)
    z = cen / spread
    for j in range(8):
        zb[j] = z[:, 128 * j:128 * j + 128].astype(bf16)

    def rows32(zl, x):
        return pl.ds(pl.multiple_of(32 * (4 * x + zl), 32), 32)

    ac = []
    for d in range(1, 16):
        t = lax.rem(me.tn + d, 16)
        ac.append(push(zb.at[t // 2], zg.at[rows32(me.zl, me.x)], as_.at[d - 1], ar.at[d - 1], t_dev[d - 1]))
    zg[rows32(me.zl, me.x), :] = zb[me.tn // 2]

    cls = lax.broadcasted_iota(jnp.int32, (NCLS, 128), 0)
    c1 = cen.astype(bf16)
    r1 = cen - c1.astype(f32)
    c2 = r1.astype(bf16)
    c3 = (r1 - c2.astype(f32)).astype(bf16)
    acc = jnp.zeros((32, NCLS), f32)
    for j in range(8):
        row = labs[2 * j, 0:1, :] + labs[2 * j + 1, 0:1, :]
        hot = (cls == row).astype(f32).astype(bf16)
        cols = slice(128 * j, 128 * j + 128)
        acc = acc + nt(c1[:, cols], hot) + nt(c2[:, cols], hot) + nt(c3[:, cols], hot)
    wall[rows32(me.zl, me.x), :] = (acc / TOKENS / spread).astype(bf16)
    lane = lax.broadcasted_iota(jnp.int32, (32, 128), 1)
    slot = 4 * me.x + me.zl
    ms[slot, :, 0:32] = jnp.where(lane < 1, mean, spread).T[0:8]
    ms[slot, :, 32:] = jnp.zeros((8, 96), f32)

    def wv(zl, x):
        return wall.at[rows32(zl, x)]

    def mv(zl, x):
        return ms.at[4 * x + zl]

    sent = gather_tensor(
        me, [(wv(me.zl, me.x), wv, ws, wr), (mv(me.zl, me.x), mv, ms_s, ms_r)]
    )
    for c in ac:
        c.wait_recv()
    sent += ac
    zz = zg[...].astype(f32)
    zz = jnp.where(lax.rem(me.tn, 2) == 1, pltpu.roll(zz, 64, 1), zz)
    zall = zz.astype(bf16)
    wt = wall[...].T
    G = jnp.dot(wt, wall[...], preferred_element_type=f32)
    C = jnp.dot(wt, zall, preferred_element_type=f32)
    gram[...] = G
    lane = lax.broadcasted_iota(jnp.int32, (128, 128), 1)
    XC[...] = jnp.where(lane < 64, C[:128], pltpu.roll(C[128:], 64, 1))
    mine = pl.ds(pl.multiple_of(16 * me.tn, 16), 16)
    XG[0:16, :] = gram[mine, 0:128]
    XG[16:32, :] = gram[mine, 128:256]
    chains = ((16, XG, RG, SG, ZG, AG, GB.at[me.tn]), (64, XC, RC, SC, ZC, AC, coords))

    def half(n, c):
        return pl.ds(pl.multiple_of(n * c, 8), n)

    cp = {}
    for i, (n, X, R, *_) in enumerate(chains):
        cp[i, 0] = push(X.at[half(n, other)], R, xs.at[i, 0], xr.at[i, 0], mate)
    for i, (n, X, R, SS, Z, *_) in enumerate(chains):
        cp[i, 0].wait_recv()
        SS[...] = X[half(n, me.core), :] + R[...]
        cp[i, 1] = push(SS, Z, xs.at[i, 1], xr.at[i, 1], across)
    for i, (n, _, _, SS, Z, A, _) in enumerate(chains):
        cp[i, 1].wait_recv()
        A[me.y] = SS[...] + Z[...]
        for k, dev in enumerate(y_dev):
            cp[i, 2 + k] = push(A.at[me.y], A.at[me.y], xs.at[i, 2 + k], xr.at[i, 2 + k], dev)

    def finish(i):
        n, A, out = chains[i][0], chains[i][5], chains[i][6]
        for k in range(3):
            cp[i, 2 + k].wait_recv()
        own = half(n, me.core)
        out[own, :] = A[0] + A[1] + A[2] + A[3]
        cp[i, 5] = push(out.at[own], out.at[own], xs.at[i, 5], xr.at[i, 5], mate)

    def gv(zl, x):
        return GB.at[4 * zl + x]

    finish(0)
    cp[0, 5].wait_recv()
    sent += gather_tensor(me, [(gv(me.zl, me.x), gv, gs, gr)])
    finish(1)
    for t in range(16):
        gram[16 * t:16 * t + 16, 0:128] = GB[t, 0:16, :]
        gram[16 * t:16 * t + 16, 128:256] = GB[t, 16:32, :]
        rowbuf[:, 32 * t:32 * t + 32] = ms[t, :, 0:32]
    cp[1, 5].wait_recv()
    coords[128:256, :] = pltpu.roll(coords[0:128, :], 64, 1)
    solved = solve(FY, gram, coords)
    fix = jnp.dot(wall[...], solved.astype(bf16), preferred_element_type=f32)
    rest = (zz - fix).T[:64]
    erased[...] = (rowbuf[0:1, :] + rowbuf[1:2, :] * rest).astype(bf16)
    for c in [*sent, *cp.values()]:
        c.wait_send()


def params(cid):
    return pltpu.CompilerParams(collective_id=cid, has_side_effects=True, vmem_limit_bytes=56 * 2**20)


DMA = pltpu.SemaphoreType.DMA
V = pltpu.VMEM
S = jax.ShapeDtypeStruct


def shards(tokens, gate_weight, up_weight, down_weight, labels):
    tn = lax.axis_index("tensor")
    twice = jnp.concatenate([labels, labels])[None, :]
    keep = (jnp.arange(128) // 64)[None, :] == tn % 2
    lab = jnp.broadcast_to(jnp.where(keep, twice, 0), (8, 128))
    nq = len(CHUNKS)
    h, labs = pl.pallas_call(
        hidden_kernel,
        out_shape=(S((UNITS, 128), bf16), S((16, 8, 128), jnp.int32)),
        in_specs=[VM, VM, ANY, ANY],
        out_specs=(VM, VM),
        scratch_shapes=[
            V((1024, 512), bf16), V((1024, 512), bf16), V((2, 2, UNITS, 512), bf16),
            V((6, 2 * UNITS, 128), bf16), V((6, 2 * UNITS, 128), bf16), V((2, 2 * UNITS, 128), f32),
            V((2 * UNITS, 256), f32), V((2 * UNITS, 128), bf16), V((2 * UNITS, 128), bf16),
            DMA((16,)), DMA((16,)), DMA((16,)), DMA((16,)), DMA((2,)), DMA((2,)), DMA((2,)),
            DMA((4,)), DMA((4,)), DMA((6, nq)), DMA((6, nq)), DMA((nq,)), DMA((nq,)),
        ],
        compiler_params=params(0),
        name="gate_up_hidden",
    )(tokens, lab, gate_weight.T, up_weight.T)
    outt = pl.pallas_call(
        down_kernel,
        out_shape=S((32, 1024), f32),
        in_specs=[VM, ANY],
        out_specs=VM,
        scratch_shapes=[
            V((2, 1024, 512), bf16), V((2, 512, 1024), bf16), V((2, 4, 1024, 256), bf16),
            V((512, 256), f32), V((4, 4, 128, 128), f32), V((4, 6, 128, 128), bf16),
            V((4, 6, 128, 128), bf16), V((4, 2, 128, 128), bf16), V((4, 3, 2, 32, 128), bf16),
            DMA((2,)), DMA((7,)), DMA((7,)), DMA((8,)), DMA((8,)),
            DMA((4, 6)), DMA((4, 6)), DMA((4, 3)), DMA((4, 3)),
        ],
        compiler_params=params(1),
        name="down_scatter",
    )(h, down_weight)
    return pl.pallas_call(
        stats_kernel,
        out_shape=S((64, 512), bf16),
        in_specs=[VM, VM],
        out_specs=VM,
        scratch_shapes=[
            V((256, 256), f32), V((256, 128), f32), V((512, 256), bf16), V((16, 8, 128), f32), V((8, 512), f32),
            V((256, 384), f32), V((8, 32, 128), bf16), V((512, 128), bf16),
            V((32, 128), f32), V((16, 128), f32), V((16, 128), f32), V((16, 128), f32), V((4, 16, 128), f32),
            V((16, 32, 128), f32),
            V((128, 128), f32), V((64, 128), f32), V((64, 128), f32), V((64, 128), f32), V((4, 64, 128), f32),
            DMA((16,)), DMA((16,)), DMA((16,)), DMA((16,)), DMA((15,)), DMA((15,)),
            DMA((2, 6)), DMA((2, 6)), DMA((16,)), DMA((16,)),
        ],
        compiler_params=params(2),
        name="stats_solve_erase",
    )(outt, labs)


def solution(mesh):
    return jax.shard_map(
        shards,
        mesh=mesh,
        in_specs=(
            P("tensor", "dp"),
            P("dp", "tensor"),
            P("dp", "tensor"),
            P("tensor", "dp"),
            P("tensor"),
        ),
        out_specs=P("tensor", "dp"),
        check_vma=False,
    )
```

```python
import functools

import jax
import jax.numpy as jnp
from jax import lax
from jax.experimental import pallas as pl
from jax.experimental.pallas import tpu as pltpu
from jax.sharding import PartitionSpec as P

MESH = pl.DeviceIdType.MESH
NCLS = 256
TOKENS = 1024
UNITS = 928
SHIFT = 920
CHUNKS = (176, 176, 176, 160, 128, 112)
HALF = 464
epsilon = 1e-05
ridge_share = 0.5
f32 = jnp.float32
bf16 = jnp.bfloat16
VM = pl.BlockSpec(memory_space=pltpu.VMEM)
ANY = pl.BlockSpec(memory_space=pl.ANY)


class Spot:
    def __init__(self):
        dp, tn = lax.axis_index("dp"), lax.axis_index("tensor")
        self.dp, self.tn = dp, tn
        self.core = lax.rem(dp, 2)
        self.zh = lax.rem(dp // 2, 2)
        self.y = dp // 4
        self.x = lax.rem(tn, 4)
        self.zl = tn // 4

    def dpid(self, y=None, zh=None, core=None):
        y = self.y if y is None else y
        zh = self.zh if zh is None else zh
        core = self.core if core is None else core
        return {"dp": y * 4 + zh * 2 + core}

    def tid(self, zl=None, x=None):
        zl = self.zl if zl is None else zl
        x = self.x if x is None else x
        return {"tensor": zl * 4 + x}


def up4(v, d):
    return lax.rem(v + d, 4)


def greet(peers):
    barrier = pltpu.get_barrier_semaphore()
    for peer in peers:
        pl.semaphore_signal(barrier, inc=1, device_id=peer, device_id_type=MESH)
    pl.semaphore_wait(barrier, len(peers))


def push(src, dst, ssem, rsem, dev):
    copy = pltpu.make_async_remote_copy(
        src_ref=src, dst_ref=dst, send_sem=ssem, recv_sem=rsem, device_id=dev, device_id_type=MESH
    )
    copy.start()
    return copy


def gather_tensor(me, parts, done=None):
    copies = []
    zc, rc, lc, fc = {}, {}, {}, {}
    right, left = up4(me.x, 1), up4(me.x, 3)
    for i, (own, block, ss, rs) in enumerate(parts):
        for d in (1, 2, 3):
            zc[i, d] = push(own, block(me.zl, me.x), ss.at[d], rs.at[d], me.tid(zl=up4(me.zl, d)))
    for d in range(4):
        z = up4(me.zl, 4 - d)
        for i, (own, block, ss, rs) in enumerate(parts):
            src = own
            if d:
                zc[i, d].wait_recv()
                src = block(z, me.x)
            rc[i, d] = push(src, block(z, me.x), ss.at[4 + d], rs.at[4 + d], me.tid(x=right))
            lc[i, d] = push(src, block(z, me.x), ss.at[8 + d], rs.at[8 + d], me.tid(x=left))
    for d in range(4):
        z = up4(me.zl, 4 - d)
        for i, (own, block, ss, rs) in enumerate(parts):
            rc[i, d].wait_recv()
            lc[i, d].wait_recv()
            if d < 2:
                v = block(z, left)
                fc[i, d] = push(v, v, ss.at[12 + d], rs.at[12 + d], me.tid(x=right))
            else:
                v = block(z, right)
                fc[i, d] = push(v, v, ss.at[12 + d], rs.at[12 + d], me.tid(x=left))
    for d in range(4):
        for i in range(len(parts)):
            fc[i, d].wait_recv()
        if done is not None:
            done(d)
    return [*zc.values(), *rc.values(), *lc.values(), *fc.values()]


def tensor_peers(me):
    peers = [me.tid(zl=up4(me.zl, d)) for d in (1, 2, 3)]
    return peers + [me.tid(x=up4(me.x, 1)), me.tid(x=up4(me.x, 3))]


def nt(a, b):
    return lax.dot_general(a, b, (((1,), (1,)), ((), ())), preferred_element_type=f32)


def hidden_kernel(tok, lab, wg, wu, h, labs, T, Tp, W, S, R, K2, PO, SZ, RZ,
                  ts, tr, ls, lr, ws, wr, wl, cs, cr, rs, rr, zs, zr):
    me = Spot()
    other = 1 - me.core
    own_rows = pl.ds(pl.multiple_of(SHIFT * me.core, 8), UNITS)
    far_rows = pl.ds(pl.multiple_of(SHIFT * other, 8), UNITS)
    local = []
    for i, w in enumerate((wg, wu)):
        c = pltpu.make_async_copy(w.at[own_rows], W.at[0, i], wl.at[i])
        c.start()
        local.append(c)
    yr, yl = up4(me.y, 1), up4(me.y, 3)
    to_r, to_l = me.dpid(y=yr), me.dpid(y=yl)
    mate = me.dpid(core=other)
    greet(tensor_peers(me) + [to_r, to_l, me.dpid(zh=1 - me.zh), mate])
    sent = []
    wx = []
    for i, w in enumerate((wg, wu)):
        wx.append(push(w.at[far_rows], W.at[1, i], ws.at[i], wr.at[i], mate))

    def tblock(zl, x):
        return T.at[pl.ds(pl.multiple_of(64 * (4 * zl + x), 64), 64)]

    def lblock(zl, x):
        return labs.at[4 * zl + x]

    T[pl.ds(pl.multiple_of(64 * me.tn, 64), 64), :] = tok[...]
    labs[me.tn] = lab[...]
    tx = []

    def share_plane(d):
        rows = pl.ds(pl.multiple_of(256 * up4(me.zl, 4 - d), 256), 256)
        tx.append(push(T.at[rows], Tp.at[rows], cs.at[d], cr.at[d], mate))

    sent += gather_tensor(me, [(tok, tblock, ts, tr), (lab, lblock, ls, lr)], share_plane)
    for c in local:
        c.wait()
    for c in wx:
        c.wait_recv()
    sent += wx + tx

    def mate_tokens(d):
        y = up4(me.y, d)
        k = up4(me.zl, 4 - y)
        rows = pl.ds(pl.multiple_of(256 * y, 256), 256)
        pltpu.make_async_remote_copy(
            src_ref=T.at[rows], dst_ref=Tp.at[rows], send_sem=cs.at[k], recv_sem=cr.at[k],
            device_id=mate, device_id_type=MESH,
        ).wait_recv()

    starts = [sum(CHUNKS[:q]) for q in range(len(CHUNKS))]

    def mult(i, q, d):
        a, n = starts[q], CHUNKS[q]
        rows = pl.ds(pl.multiple_of(256 * up4(me.y, d), 256), 256)
        return nt(W[0, i, a:a + n, :], T[rows, :]) + nt(W[1, i, a:a + n, :], Tp[rows, :])

    cps = {}

    def send(k, q, dev):
        rows = pl.ds(2 * starts[q], 2 * CHUNKS[q])
        cps[k, q] = push(S.at[k, rows], R.at[k, rows], rs.at[k, q], rr.at[k, q], dev)

    def first(q):
        a, n = starts[q], CHUNKS[q]
        if q == 0:
            mate_tokens(2)
        for i in range(2):
            o = 2 * a + i * n
            p = mult(i, q, 2)
            S[0, o:o + n, :] = p[:, :128].astype(bf16)
            S[1, o:o + n, :] = p[:, 128:].astype(bf16)
        send(0, q, to_r)
        send(1, q, to_l)
        if q == 0:
            mate_tokens(1)
        for i in range(2):
            o = 2 * a + i * n
            p = mult(i, q, 1)
            K2[0, o:o + n, :] = p[:, :128]
            S[3, o:o + n, :] = p[:, 128:].astype(bf16)
        send(3, q, to_r)
        if q == 0:
            mate_tokens(3)
        for i in range(2):
            o = 2 * a + i * n
            p = mult(i, q, 3)
            K2[1, o:o + n, :] = p[:, 128:]
            S[4, o:o + n, :] = p[:, :128].astype(bf16)
        send(4, q, to_l)
        if q == 0:
            mate_tokens(0)
        for i in range(2):
            o = 2 * a + i * n
            PO[o:o + n, :] = mult(i, q, 0)

    def second(q):
        o, n = 2 * starts[q], 2 * CHUNKS[q]
        cps[0, q].wait_recv()
        S[2, o:o + n, :] = (K2[0, o:o + n, :] + R[0, o:o + n, :].astype(f32)).astype(bf16)
        send(2, q, to_r)
        cps[1, q].wait_recv()
        S[5, o:o + n, :] = (K2[1, o:o + n, :] + R[1, o:o + n, :].astype(f32)).astype(bf16)
        send(5, q, to_l)

    zc = {}

    def third(q):
        o, n = 2 * starts[q], 2 * CHUNKS[q]
        for k in (2, 3, 4, 5):
            cps[k, q].wait_recv()
        a = PO[o:o + n, :128] + R[2, o:o + n, :].astype(f32) + R[4, o:o + n, :].astype(f32)
        b = PO[o:o + n, 128:] + R[3, o:o + n, :].astype(f32) + R[5, o:o + n, :].astype(f32)
        low = me.zh == 0
        SZ[o:o + n, :] = jnp.where(low, b, a).astype(bf16)
        PO[o:o + n, :128] = jnp.where(low, a, b)
        rows = pl.ds(o, n)
        zc[q] = push(SZ.at[rows], RZ.at[rows], zs.at[q], zr.at[q], me.dpid(zh=1 - me.zh))

    def last(q):
        a, n = starts[q], CHUNKS[q]
        o = 2 * a
        zc[q].wait_recv()
        tot = PO[o:o + 2 * n, :128] + RZ[o:o + 2 * n, :].astype(f32)
        g, u = tot[:n], tot[n:]
        h[a:a + n, :] = (g / (1.0 + jnp.exp(-g)) * u).astype(bf16)

    nq = len(CHUNKS)
    for i in range(nq + 2):
        if i < nq:
            first(i)
        if 1 <= i <= nq:
            second(i - 1)
        if i >= 2:
            third(i - 2)
    for q in range(nq):
        last(q)
    for c in [*sent, *cps.values(), *zc.values()]:
        c.wait_send()


def down_kernel(h, down, outt, D, DT, H, PG, KO, SO, RO, SZ, RZ,
                dl, hs, hr, cs, cr, os, orr, zs, zr):
    me = Spot()
    other = 1 - me.core
    loads = []
    for i, c in enumerate((me.core, other)):
        cp = pltpu.make_async_copy(
            down.at[pl.ds(pl.multiple_of(SHIFT * c, 8), UNITS)], D.at[i, pl.ds(0, UNITS)], dl.at[i]
        )
        cp.start()
        loads.append(cp)
    yr, yl, yf = up4(me.y, 1), up4(me.y, 3), up4(me.y, 2)
    to_r, to_l = me.dpid(y=yr), me.dpid(y=yl)
    mate = me.dpid(core=other)
    across = me.dpid(zh=1 - me.zh)
    xr, xl = me.tid(x=up4(me.x, 1)), me.tid(x=up4(me.x, 3))
    greet(tensor_peers(me) + [to_r, to_l, across, mate])

    def hv(i, y, zh, p):
        return H.at[i, y, pl.ds(HALF * p, HALF), pl.ds(pl.multiple_of(128 * zh, 128), 128)]

    def own(p):
        return h.at[pl.ds(HALF * p, HALF)]

    zh, zo = me.zh, 1 - me.zh
    sent = []
    hc, cc = {}, {}

    def move(k, p, src, y, z, dev):
        hc[k, p] = push(src, hv(0, y, z, p), hs.at[k, p], hr.at[k, p], dev)

    def share(k, p, src, y, z):
        cc[k, p] = push(src, hv(1, y, z, p), cs.at[k, p], cr.at[k, p], mate)
        sent.append(cc[k, p])

    def landed(*ks):
        for k in ks:
            for p in range(2):
                cc[k, p].wait_recv()

    for p in range(2):
        move(0, p, own(p), me.y, zh, across)
        move(1, p, own(p), me.y, zh, to_r)
        move(2, p, own(p), me.y, zh, to_l)
    for p in range(2):
        share(0, p, own(p), me.y, zh)
    H[0, me.y, 0:UNITS, pl.ds(pl.multiple_of(128 * zh, 128), 128)] = h[...]
    H[:, :, UNITS:, :] = jnp.zeros((2, 4, 1024 - UNITS, 256), bf16)
    for i in range(2):
        loads[i].wait()
        D[i, UNITS:, :] = jnp.zeros((1024 - UNITS, 512), bf16)
        dup = (me.core if i == 0 else other) == 1
        head = D[i, 0:16, :].astype(f32)
        row = lax.broadcasted_iota(jnp.int32, head.shape, 0)
        D[i, 0:16, :] = jnp.where(jnp.logical_and(dup, row < 8), 0.0, head).astype(bf16)
        for k in range(4):
            DT[i, :, 256 * k:256 * k + 256] = D[i, 256 * k:256 * k + 256, :].T
    for p in range(2):
        hc[1, p].wait_recv()
        v = hv(0, yl, zh, p)
        move(5, p, v, yl, zh, to_r)
        share(2, p, v, yl, zh)
        hc[2, p].wait_recv()
        share(3, p, hv(0, yr, zh, p), yr, zh)
    for p in range(2):
        hc[0, p].wait_recv()
        v = hv(0, me.y, zo, p)
        move(3, p, v, me.y, zo, to_r)
        move(4, p, v, me.y, zo, to_l)
        share(1, p, v, me.y, zo)

    oc = {}

    def osend(g, k, dev):
        oc[g, k] = push(SO.at[g, k], RO.at[g, k], os.at[g, k], orr.at[g, k], dev)

    def rows(d):
        return pl.ds(pl.multiple_of(128 * up4(me.x, d), 128), 128)

    def group(g, y):
        PG[...] = jnp.dot(DT[0], H[0, y], preferred_element_type=f32) + jnp.dot(
            DT[1], H[1, y], preferred_element_type=f32
        )
        SO[g, 0] = PG[rows(2), 0:128].astype(bf16)
        SO[g, 1] = PG[rows(2), 128:256].astype(bf16)
        osend(g, 0, xr)
        osend(g, 1, xl)
        SO[g, 3] = PG[rows(1), 128:256].astype(bf16)
        osend(g, 3, xr)
        SO[g, 4] = PG[rows(3), 0:128].astype(bf16)
        osend(g, 4, xl)
        KO[g, 0] = PG[rows(1), 0:128]
        KO[g, 1] = PG[rows(3), 128:256]
        KO[g, 2] = PG[rows(0), 0:128]
        KO[g, 3] = PG[rows(0), 128:256]

    def relay(g):
        oc[g, 0].wait_recv()
        SO[g, 2] = (KO[g, 0] + RO[g, 0].astype(f32)).astype(bf16)
        osend(g, 2, xr)
        oc[g, 1].wait_recv()
        SO[g, 5] = (KO[g, 1] + RO[g, 1].astype(f32)).astype(bf16)
        osend(g, 5, xl)

    zc = {}

    def settle(g):
        for k in (2, 3, 4, 5):
            oc[g, k].wait_recv()
        KO[g, 2] = KO[g, 2] + RO[g, 2].astype(f32) + RO[g, 4].astype(f32)
        KO[g, 3] = KO[g, 3] + RO[g, 3].astype(f32) + RO[g, 5].astype(f32)
        SZ[g, 0] = KO[g, 2].astype(bf16)
        SZ[g, 1] = KO[g, 3].astype(bf16)
        for d in (1, 2, 3):
            z = up4(me.zl, d)
            part = pl.ds(pl.multiple_of(32 * z, 32), 32)
            zc[g, d] = push(
                SZ.at[g, pl.ds(0, 2), part], RZ.at[g, d - 1], zs.at[g, d - 1], zr.at[g, d - 1], me.tid(zl=z)
            )

    def close(g, y):
        mine = pl.ds(pl.multiple_of(32 * me.zl, 32), 32)
        for d in (1, 2, 3):
            zc[g, d].wait_recv()
        for b in range(2):
            tot = KO[g, 2 + b, mine, :]
            for d in range(3):
                tot = tot + RZ[g, d, b].astype(f32)
            outt[:, pl.ds(pl.multiple_of(256 * y + 128 * b, 128), 128)] = tot

    landed(0, 1)
    group(0, me.y)
    for p in range(2):
        hc[4, p].wait_recv()
        v = hv(0, yr, zo, p)
        move(6, p, v, yr, zo, to_l)
        share(4, p, v, yr, zo)
        hc[3, p].wait_recv()
        share(5, p, hv(0, yl, zo, p), yl, zo)
    landed(3, 4)
    group(1, yr)
    relay(0)
    landed(2, 5)
    group(2, yl)
    relay(1)
    for p in range(2):
        hc[5, p].wait_recv()
        share(6, p, hv(0, yf, zh, p), yf, zh)
    settle(0)
    for p in range(2):
        hc[6, p].wait_recv()
        share(7, p, hv(0, yf, zo, p), yf, zo)
    landed(6, 7)
    group(3, yf)
    relay(2)
    settle(1)
    relay(3)
    settle(2)
    close(0, me.y)
    settle(3)
    close(1, yr)
    close(2, yl)
    close(3, yf)
    for c in [*sent, *hc.values(), *oc.values(), *zc.values()]:
        c.wait_send()


def scales():
    low, out = 1.0 / 513.0, []
    for _ in range(8):
        out.append(2.0 / (1.0 + low))
        low = 4.0 * low / (1.0 + low) ** 2
    return out


def solve(FY, gram, coords):
    sc = scales()
    eye = lax.broadcasted_iota(jnp.int32, (NCLS, NCLS), 0) == lax.broadcasted_iota(jnp.int32, (NCLS, NCLS), 1)
    G = gram[...]
    diag = jnp.where(eye, G, 0.0)
    trace = jnp.sum(jnp.sum(diag, axis=1, keepdims=True), axis=0, keepdims=True)
    ridge = ridge_share * trace / NCLS
    inv = 1.0 / (513.0 * ridge)
    FY[:, :NCLS] = jnp.where(eye, 1.0 - sc[0] / 513.0, 0.0) - (sc[0] * inv) * G
    FY[:, NCLS:] = coords[...]

    def pick(k, vals):
        out = jnp.float32(vals[0])
        for i in range(1, len(vals)):
            out = jnp.where(k == i, jnp.float32(vals[i]), out)
        return out

    def step(k, carry):
        now, nxt = pick(k, sc[:7]), pick(k, sc[1:])
        both = jnp.dot(FY[:, :NCLS], FY[...], precision=lax.Precision.HIGHEST, preferred_element_type=f32)
        FY[:, NCLS:] = now * (FY[:, NCLS:] + both[:, NCLS:])
        FY[:, :NCLS] = nxt * both[:, :NCLS] + jnp.where(eye, 1.0 - nxt, 0.0)
        return carry

    lax.fori_loop(0, 7, step, 0)
    Y = FY[:, NCLS:]
    last = jnp.dot(FY[:, :NCLS], Y, precision=lax.Precision.HIGHEST, preferred_element_type=f32)
    return (sc[7] * inv) * (Y + last)


def stats_kernel(outt, labs, erased, gram, coords, wall, ms, rowbuf, FY,
                 zb, zg, XG, RG, SG, ZG, AG, GB, XC, RC, SC, ZC, AC,
                 ws, wr, ms_s, ms_r, as_, ar, xs, xr, gs, gr):
    me = Spot()
    other = 1 - me.core
    mate = me.dpid(core=other)
    across = me.dpid(zh=1 - me.zh)
    y_dev = [me.dpid(y=up4(me.y, d)) for d in (1, 2, 3)]
    t_dev = [{"tensor": lax.rem(me.tn + d, 16)} for d in range(1, 16)]
    greet(t_dev + y_dev + [across, mate])

    out = outt[...]
    mean = jnp.sum(out, axis=1, keepdims=True) / TOKENS
    cen = out - mean
    spread = jnp.sqrt(jnp.sum(cen * cen, axis=1, keepdims=True) / TOKENS + epsilon)
    z = cen / spread
    for j in range(8):
        zb[j] = z[:, 128 * j:128 * j + 128].astype(bf16)

    def rows32(zl, x):
        return pl.ds(pl.multiple_of(32 * (4 * x + zl), 32), 32)

    ac = []
    for d in range(1, 16):
        t = lax.rem(me.tn + d, 16)
        ac.append(push(zb.at[t // 2], zg.at[rows32(me.zl, me.x)], as_.at[d - 1], ar.at[d - 1], t_dev[d - 1]))
    zg[rows32(me.zl, me.x), :] = zb[me.tn // 2]

    cls = lax.broadcasted_iota(jnp.int32, (NCLS, 128), 0)
    c1 = cen.astype(bf16)
    r1 = cen - c1.astype(f32)
    c2 = r1.astype(bf16)
    c3 = (r1 - c2.astype(f32)).astype(bf16)
    acc = jnp.zeros((32, NCLS), f32)
    for j in range(8):
        row = labs[2 * j, 0:1, :] + labs[2 * j + 1, 0:1, :]
        hot = (cls == row).astype(f32).astype(bf16)
        cols = slice(128 * j, 128 * j + 128)
        acc = acc + nt(c1[:, cols], hot) + nt(c2[:, cols], hot) + nt(c3[:, cols], hot)
    wall[rows32(me.zl, me.x), :] = (acc / TOKENS / spread).astype(bf16)
    lane = lax.broadcasted_iota(jnp.int32, (32, 128), 1)
    slot = 4 * me.x + me.zl
    ms[slot, :, 0:32] = jnp.where(lane < 1, mean, spread).T[0:8]
    ms[slot, :, 32:] = jnp.zeros((8, 96), f32)

    def wv(zl, x):
        return wall.at[rows32(zl, x)]

    def mv(zl, x):
        return ms.at[4 * x + zl]

    sent = gather_tensor(
        me, [(wv(me.zl, me.x), wv, ws, wr), (mv(me.zl, me.x), mv, ms_s, ms_r)]
    )
    for c in ac:
        c.wait_recv()
    sent += ac
    zz = zg[...].astype(f32)
    zz = jnp.where(lax.rem(me.tn, 2) == 1, pltpu.roll(zz, 64, 1), zz)
    zall = zz.astype(bf16)
    wt = wall[...].T
    G = jnp.dot(wt, wall[...], preferred_element_type=f32)
    C = jnp.dot(wt, zall, preferred_element_type=f32)
    gram[...] = G
    lane = lax.broadcasted_iota(jnp.int32, (128, 128), 1)
    XC[...] = jnp.where(lane < 64, C[:128], pltpu.roll(C[128:], 64, 1))
    mine = pl.ds(pl.multiple_of(16 * me.tn, 16), 16)
    XG[0:16, :] = gram[mine, 0:128]
    XG[16:32, :] = gram[mine, 128:256]
    chains = ((16, XG, RG, SG, ZG, AG, GB.at[me.tn]), (64, XC, RC, SC, ZC, AC, coords))

    def half(n, c):
        return pl.ds(pl.multiple_of(n * c, 8), n)

    cp = {}
    for i, (n, X, R, *_) in enumerate(chains):
        cp[i, 0] = push(X.at[half(n, other)], R, xs.at[i, 0], xr.at[i, 0], mate)
    for i, (n, X, R, SS, Z, *_) in enumerate(chains):
        cp[i, 0].wait_recv()
        SS[...] = X[half(n, me.core), :] + R[...]
        cp[i, 1] = push(SS, Z, xs.at[i, 1], xr.at[i, 1], across)
    for i, (n, _, _, SS, Z, A, _) in enumerate(chains):
        cp[i, 1].wait_recv()
        A[me.y] = SS[...] + Z[...]
        for k, dev in enumerate(y_dev):
            cp[i, 2 + k] = push(A.at[me.y], A.at[me.y], xs.at[i, 2 + k], xr.at[i, 2 + k], dev)

    def finish(i):
        n, A, out = chains[i][0], chains[i][5], chains[i][6]
        for k in range(3):
            cp[i, 2 + k].wait_recv()
        own = half(n, me.core)
        out[own, :] = A[0] + A[1] + A[2] + A[3]
        cp[i, 5] = push(out.at[own], out.at[own], xs.at[i, 5], xr.at[i, 5], mate)

    def gv(zl, x):
        return GB.at[4 * zl + x]

    finish(0)
    cp[0, 5].wait_recv()
    sent += gather_tensor(me, [(gv(me.zl, me.x), gv, gs, gr)])
    finish(1)
    for t in range(16):
        gram[16 * t:16 * t + 16, 0:128] = GB[t, 0:16, :]
        gram[16 * t:16 * t + 16, 128:256] = GB[t, 16:32, :]
        rowbuf[:, 32 * t:32 * t + 32] = ms[t, :, 0:32]
    cp[1, 5].wait_recv()
    coords[128:256, :] = pltpu.roll(coords[0:128, :], 64, 1)
    solved = solve(FY, gram, coords)
    fix = jnp.dot(wall[...], solved.astype(bf16), preferred_element_type=f32)
    rest = (zz - fix).T[:64]
    erased[...] = (rowbuf[0:1, :] + rowbuf[1:2, :] * rest).astype(bf16)
    for c in [*sent, *cp.values()]:
        c.wait_send()


def params(cid):
    return pltpu.CompilerParams(collective_id=cid, has_side_effects=True, vmem_limit_bytes=56 * 2**20)


DMA = pltpu.SemaphoreType.DMA
V = pltpu.VMEM
S = jax.ShapeDtypeStruct


def shards(tokens, gate_weight, up_weight, down_weight, labels):
    tn = lax.axis_index("tensor")
    twice = jnp.concatenate([labels, labels])[None, :]
    keep = (jnp.arange(128) // 64)[None, :] == tn % 2
    lab = jnp.broadcast_to(jnp.where(keep, twice, 0), (8, 128))
    nq = len(CHUNKS)
    h, labs = pl.pallas_call(
        hidden_kernel,
        out_shape=(S((UNITS, 128), bf16), S((16, 8, 128), jnp.int32)),
        in_specs=[VM, VM, ANY, ANY],
        out_specs=(VM, VM),
        scratch_shapes=[
            V((1024, 512), bf16), V((1024, 512), bf16), V((2, 2, UNITS, 512), bf16),
            V((6, 2 * UNITS, 128), bf16), V((6, 2 * UNITS, 128), bf16), V((2, 2 * UNITS, 128), f32),
            V((2 * UNITS, 256), f32), V((2 * UNITS, 128), bf16), V((2 * UNITS, 128), bf16),
            DMA((16,)), DMA((16,)), DMA((16,)), DMA((16,)), DMA((2,)), DMA((2,)), DMA((2,)),
            DMA((4,)), DMA((4,)), DMA((6, nq)), DMA((6, nq)), DMA((nq,)), DMA((nq,)),
        ],
        compiler_params=params(0),
        name="gate_up_hidden",
    )(tokens, lab, gate_weight.T, up_weight.T)
    outt = pl.pallas_call(
        down_kernel,
        out_shape=S((32, 1024), f32),
        in_specs=[VM, ANY],
        out_specs=VM,
        scratch_shapes=[
            V((2, 1024, 512), bf16), V((2, 512, 1024), bf16), V((2, 4, 1024, 256), bf16),
            V((512, 256), f32), V((4, 4, 128, 128), f32), V((4, 6, 128, 128), bf16),
            V((4, 6, 128, 128), bf16), V((4, 2, 128, 128), bf16), V((4, 3, 2, 32, 128), bf16),
            DMA((2,)), DMA((7, 2)), DMA((7, 2)), DMA((8, 2)), DMA((8, 2)),
            DMA((4, 6)), DMA((4, 6)), DMA((4, 3)), DMA((4, 3)),
        ],
        compiler_params=params(1),
        name="down_scatter",
    )(h, down_weight)
    return pl.pallas_call(
        stats_kernel,
        out_shape=S((64, 512), bf16),
        in_specs=[VM, VM],
        out_specs=VM,
        scratch_shapes=[
            V((256, 256), f32), V((256, 128), f32), V((512, 256), bf16), V((16, 8, 128), f32), V((8, 512), f32),
            V((256, 384), f32), V((8, 32, 128), bf16), V((512, 128), bf16),
            V((32, 128), f32), V((16, 128), f32), V((16, 128), f32), V((16, 128), f32), V((4, 16, 128), f32),
            V((16, 32, 128), f32),
            V((128, 128), f32), V((64, 128), f32), V((64, 128), f32), V((64, 128), f32), V((4, 64, 128), f32),
            DMA((16,)), DMA((16,)), DMA((16,)), DMA((16,)), DMA((15,)), DMA((15,)),
            DMA((2, 6)), DMA((2, 6)), DMA((16,)), DMA((16,)),
        ],
        compiler_params=params(2),
        name="stats_solve_erase",
    )(outt, labs)


def solution(mesh):
    return jax.shard_map(
        shards,
        mesh=mesh,
        in_specs=(
            P("tensor", "dp"),
            P("dp", "tensor"),
            P("dp", "tensor"),
            P("tensor", "dp"),
            P("tensor"),
        ),
        out_specs=P("tensor", "dp"),
        check_vma=False,
    )
```

```python
import functools

import jax
import jax.numpy as jnp
from jax import lax
from jax.experimental import pallas as pl
from jax.experimental.pallas import tpu as pltpu
from jax.sharding import PartitionSpec as P

MESH = pl.DeviceIdType.MESH
NCLS = 256
TOKENS = 1024
UNITS = 928
SHIFT = 920
CHUNKS = (160, 144, 128, 128, 112, 96, 80, 80)
EDGES = (0, 240, 480, 704, 928)
epsilon = 1e-05
ridge_share = 0.5
f32 = jnp.float32
bf16 = jnp.bfloat16
VM = pl.BlockSpec(memory_space=pltpu.VMEM)
ANY = pl.BlockSpec(memory_space=pl.ANY)


class Spot:
    def __init__(self):
        dp, tn = lax.axis_index("dp"), lax.axis_index("tensor")
        self.dp, self.tn = dp, tn
        self.core = lax.rem(dp, 2)
        self.zh = lax.rem(dp // 2, 2)
        self.y = dp // 4
        self.x = lax.rem(tn, 4)
        self.zl = tn // 4

    def dpid(self, y=None, zh=None, core=None):
        y = self.y if y is None else y
        zh = self.zh if zh is None else zh
        core = self.core if core is None else core
        return {"dp": y * 4 + zh * 2 + core}

    def tid(self, zl=None, x=None):
        zl = self.zl if zl is None else zl
        x = self.x if x is None else x
        return {"tensor": zl * 4 + x}


def up4(v, d):
    return lax.rem(v + d, 4)


def greet(peers):
    barrier = pltpu.get_barrier_semaphore()
    for peer in peers:
        pl.semaphore_signal(barrier, inc=1, device_id=peer, device_id_type=MESH)
    pl.semaphore_wait(barrier, len(peers))


def push(src, dst, ssem, rsem, dev):
    copy = pltpu.make_async_remote_copy(
        src_ref=src, dst_ref=dst, send_sem=ssem, recv_sem=rsem, device_id=dev, device_id_type=MESH
    )
    copy.start()
    return copy


def gather_tensor(me, parts, done=None):
    copies = []
    zc, rc, lc, fc = {}, {}, {}, {}
    right, left = up4(me.x, 1), up4(me.x, 3)
    for i, (own, block, ss, rs) in enumerate(parts):
        for d in (1, 2, 3):
            zc[i, d] = push(own, block(me.zl, me.x), ss.at[d], rs.at[d], me.tid(zl=up4(me.zl, d)))
    for d in range(4):
        z = up4(me.zl, 4 - d)
        for i, (own, block, ss, rs) in enumerate(parts):
            src = own
            if d:
                zc[i, d].wait_recv()
                src = block(z, me.x)
            rc[i, d] = push(src, block(z, me.x), ss.at[4 + d], rs.at[4 + d], me.tid(x=right))
            lc[i, d] = push(src, block(z, me.x), ss.at[8 + d], rs.at[8 + d], me.tid(x=left))
    for d in range(4):
        z = up4(me.zl, 4 - d)
        for i, (own, block, ss, rs) in enumerate(parts):
            rc[i, d].wait_recv()
            lc[i, d].wait_recv()
            if d < 2:
                v = block(z, left)
                fc[i, d] = push(v, v, ss.at[12 + d], rs.at[12 + d], me.tid(x=right))
            else:
                v = block(z, right)
                fc[i, d] = push(v, v, ss.at[12 + d], rs.at[12 + d], me.tid(x=left))
    for d in range(4):
        for i in range(len(parts)):
            fc[i, d].wait_recv()
        if done is not None:
            done(d)
    return [*zc.values(), *rc.values(), *lc.values(), *fc.values()]


def tensor_peers(me):
    peers = [me.tid(zl=up4(me.zl, d)) for d in (1, 2, 3)]
    return peers + [me.tid(x=up4(me.x, 1)), me.tid(x=up4(me.x, 3))]


def nt(a, b):
    return lax.dot_general(a, b, (((1,), (1,)), ((), ())), preferred_element_type=f32)


def hidden_kernel(tok, lab, wg, wu, h, labs, T, Tp, W, S, R, K2, PO, SZ, RZ,
                  ts, tr, ls, lr, ws, wr, wl, cs, cr, rs, rr, zs, zr):
    me = Spot()
    other = 1 - me.core
    own_rows = pl.ds(pl.multiple_of(SHIFT * me.core, 8), UNITS)
    far_rows = pl.ds(pl.multiple_of(SHIFT * other, 8), UNITS)
    local = []
    for i, w in enumerate((wg, wu)):
        c = pltpu.make_async_copy(w.at[own_rows], W.at[0, i], wl.at[i])
        c.start()
        local.append(c)
    yr, yl = up4(me.y, 1), up4(me.y, 3)
    to_r, to_l = me.dpid(y=yr), me.dpid(y=yl)
    mate = me.dpid(core=other)
    greet(tensor_peers(me) + [to_r, to_l, me.dpid(zh=1 - me.zh), mate])
    sent = []
    wx = []
    for i, w in enumerate((wg, wu)):
        wx.append(push(w.at[far_rows], W.at[1, i], ws.at[i], wr.at[i], mate))

    def tblock(zl, x):
        return T.at[pl.ds(pl.multiple_of(64 * (4 * zl + x), 64), 64)]

    def lblock(zl, x):
        return labs.at[4 * zl + x]

    T[pl.ds(pl.multiple_of(64 * me.tn, 64), 64), :] = tok[...]
    labs[me.tn] = lab[...]
    tx = []

    def share_plane(d):
        rows = pl.ds(pl.multiple_of(256 * up4(me.zl, 4 - d), 256), 256)
        tx.append(push(T.at[rows], Tp.at[rows], cs.at[d], cr.at[d], mate))

    sent += gather_tensor(me, [(tok, tblock, ts, tr), (lab, lblock, ls, lr)], share_plane)
    for c in local:
        c.wait()
    for c in wx:
        c.wait_recv()
    sent += wx + tx

    def mate_tokens(d):
        y = up4(me.y, d)
        k = up4(me.zl, 4 - y)
        rows = pl.ds(pl.multiple_of(256 * y, 256), 256)
        pltpu.make_async_remote_copy(
            src_ref=T.at[rows], dst_ref=Tp.at[rows], send_sem=cs.at[k], recv_sem=cr.at[k],
            device_id=mate, device_id_type=MESH,
        ).wait_recv()

    starts = [sum(CHUNKS[:q]) for q in range(len(CHUNKS))]

    def mult(i, q, d):
        a, n = starts[q], CHUNKS[q]
        rows = pl.ds(pl.multiple_of(256 * up4(me.y, d), 256), 256)
        return nt(W[0, i, a:a + n, :], T[rows, :]) + nt(W[1, i, a:a + n, :], Tp[rows, :])

    cps = {}

    def send(k, q, dev):
        rows = pl.ds(2 * starts[q], 2 * CHUNKS[q])
        cps[k, q] = push(S.at[k, rows], R.at[k, rows], rs.at[k, q], rr.at[k, q], dev)

    def first(q):
        a, n = starts[q], CHUNKS[q]
        if q == 0:
            mate_tokens(2)
        for i in range(2):
            o = 2 * a + i * n
            p = mult(i, q, 2)
            S[0, o:o + n, :] = p[:, :128].astype(bf16)
            S[1, o:o + n, :] = p[:, 128:].astype(bf16)
        send(0, q, to_r)
        send(1, q, to_l)
        if q == 0:
            mate_tokens(1)
        for i in range(2):
            o = 2 * a + i * n
            p = mult(i, q, 1)
            K2[0, o:o + n, :] = p[:, :128]
            S[3, o:o + n, :] = p[:, 128:].astype(bf16)
        send(3, q, to_r)
        if q == 0:
            mate_tokens(3)
        for i in range(2):
            o = 2 * a + i * n
            p = mult(i, q, 3)
            K2[1, o:o + n, :] = p[:, 128:]
            S[4, o:o + n, :] = p[:, :128].astype(bf16)
        send(4, q, to_l)
        if q == 0:
            mate_tokens(0)
        for i in range(2):
            o = 2 * a + i * n
            PO[o:o + n, :] = mult(i, q, 0)

    def second(q):
        o, n = 2 * starts[q], 2 * CHUNKS[q]
        cps[0, q].wait_recv()
        S[2, o:o + n, :] = (K2[0, o:o + n, :] + R[0, o:o + n, :].astype(f32)).astype(bf16)
        send(2, q, to_r)
        cps[1, q].wait_recv()
        S[5, o:o + n, :] = (K2[1, o:o + n, :] + R[1, o:o + n, :].astype(f32)).astype(bf16)
        send(5, q, to_l)

    zc = {}

    def third(q):
        o, n = 2 * starts[q], 2 * CHUNKS[q]
        for k in (2, 3, 4, 5):
            cps[k, q].wait_recv()
        a = PO[o:o + n, :128] + R[2, o:o + n, :].astype(f32) + R[4, o:o + n, :].astype(f32)
        b = PO[o:o + n, 128:] + R[3, o:o + n, :].astype(f32) + R[5, o:o + n, :].astype(f32)
        low = me.zh == 0
        SZ[o:o + n, :] = jnp.where(low, b, a).astype(bf16)
        PO[o:o + n, :128] = jnp.where(low, a, b)
        rows = pl.ds(o, n)
        zc[q] = push(SZ.at[rows], RZ.at[rows], zs.at[q], zr.at[q], me.dpid(zh=1 - me.zh))

    def last(q):
        a, n = starts[q], CHUNKS[q]
        o = 2 * a
        zc[q].wait_recv()
        tot = PO[o:o + 2 * n, :128] + RZ[o:o + 2 * n, :].astype(f32)
        g, u = tot[:n], tot[n:]
        h[a:a + n, :] = (g / (1.0 + jnp.exp(-g)) * u).astype(bf16)

    nq = len(CHUNKS)
    for i in range(nq + 2):
        if i < nq:
            first(i)
        if 1 <= i <= nq:
            second(i - 1)
        if i >= 2:
            third(i - 2)
        if i >= 4:
            last(i - 4)
    for q in range(nq - 2, nq):
        last(q)
    for c in [*sent, *cps.values(), *zc.values()]:
        c.wait_send()


def down_kernel(h, down, outt, D, DT, H, PG, KO, SO, RO, SZ, RZ,
                dl, hs, hr, cs, cr, os, orr, zs, zr):
    me = Spot()
    other = 1 - me.core
    loads = []
    for i, c in enumerate((me.core, other)):
        cp = pltpu.make_async_copy(
            down.at[pl.ds(pl.multiple_of(SHIFT * c, 8), UNITS)], D.at[i, pl.ds(0, UNITS)], dl.at[i]
        )
        cp.start()
        loads.append(cp)
    yr, yl, yf = up4(me.y, 1), up4(me.y, 3), up4(me.y, 2)
    to_r, to_l = me.dpid(y=yr), me.dpid(y=yl)
    mate = me.dpid(core=other)
    across = me.dpid(zh=1 - me.zh)
    xr, xl = me.tid(x=up4(me.x, 1)), me.tid(x=up4(me.x, 3))
    greet(tensor_peers(me) + [to_r, to_l, across, mate])

    def hv(i, y, zh, p):
        return H.at[i, y, pl.ds(EDGES[p], EDGES[p + 1] - EDGES[p]), pl.ds(pl.multiple_of(128 * zh, 128), 128)]

    def own(p):
        return h.at[pl.ds(EDGES[p], EDGES[p + 1] - EDGES[p])]

    zh, zo = me.zh, 1 - me.zh
    sent = []
    hc, cc = {}, {}

    def move(k, p, src, y, z, dev):
        hc[k, p] = push(src, hv(0, y, z, p), hs.at[k, p], hr.at[k, p], dev)

    def share(k, p, src, y, z):
        cc[k, p] = push(src, hv(1, y, z, p), cs.at[k, p], cr.at[k, p], mate)
        sent.append(cc[k, p])

    def landed(*ks):
        for k in ks:
            for p in range(4):
                cc[k, p].wait_recv()

    for p in range(4):
        move(0, p, own(p), me.y, zh, across)
        move(1, p, own(p), me.y, zh, to_r)
        move(2, p, own(p), me.y, zh, to_l)
    for p in range(4):
        share(0, p, own(p), me.y, zh)
    H[0, me.y, 0:UNITS, pl.ds(pl.multiple_of(128 * zh, 128), 128)] = h[...]
    H[:, :, UNITS:, :] = jnp.zeros((2, 4, 1024 - UNITS, 256), bf16)
    for i in range(2):
        loads[i].wait()
        D[i, UNITS:, :] = jnp.zeros((1024 - UNITS, 512), bf16)
        dup = (me.core if i == 0 else other) == 1
        head = D[i, 0:16, :].astype(f32)
        row = lax.broadcasted_iota(jnp.int32, head.shape, 0)
        D[i, 0:16, :] = jnp.where(jnp.logical_and(dup, row < 8), 0.0, head).astype(bf16)
        for k in range(4):
            DT[i, :, 256 * k:256 * k + 256] = D[i, 256 * k:256 * k + 256, :].T
    for p in range(4):
        hc[1, p].wait_recv()
        v = hv(0, yl, zh, p)
        move(5, p, v, yl, zh, to_r)
        share(2, p, v, yl, zh)
        hc[2, p].wait_recv()
        share(3, p, hv(0, yr, zh, p), yr, zh)
    for p in range(4):
        hc[0, p].wait_recv()
        v = hv(0, me.y, zo, p)
        move(3, p, v, me.y, zo, to_r)
        move(4, p, v, me.y, zo, to_l)
        share(1, p, v, me.y, zo)

    oc = {}

    def osend(g, k, dev):
        oc[g, k] = push(SO.at[g, k], RO.at[g, k], os.at[g, k], orr.at[g, k], dev)

    def rows(d):
        return pl.ds(pl.multiple_of(128 * up4(me.x, d), 128), 128)

    def group(g, y):
        PG[...] = jnp.dot(DT[0], H[0, y], preferred_element_type=f32) + jnp.dot(
            DT[1], H[1, y], preferred_element_type=f32
        )
        SO[g, 0] = PG[rows(2), 0:128].astype(bf16)
        SO[g, 1] = PG[rows(2), 128:256].astype(bf16)
        osend(g, 0, xr)
        osend(g, 1, xl)
        SO[g, 3] = PG[rows(1), 128:256].astype(bf16)
        osend(g, 3, xr)
        SO[g, 4] = PG[rows(3), 0:128].astype(bf16)
        osend(g, 4, xl)
        KO[g, 0] = PG[rows(1), 0:128]
        KO[g, 1] = PG[rows(3), 128:256]
        KO[g, 2] = PG[rows(0), 0:128]
        KO[g, 3] = PG[rows(0), 128:256]

    def relay(g):
        oc[g, 0].wait_recv()
        SO[g, 2] = (KO[g, 0] + RO[g, 0].astype(f32)).astype(bf16)
        osend(g, 2, xr)
        oc[g, 1].wait_recv()
        SO[g, 5] = (KO[g, 1] + RO[g, 1].astype(f32)).astype(bf16)
        osend(g, 5, xl)

    zc = {}

    def settle(g):
        for k in (2, 3, 4, 5):
            oc[g, k].wait_recv()
        KO[g, 2] = KO[g, 2] + RO[g, 2].astype(f32) + RO[g, 4].astype(f32)
        KO[g, 3] = KO[g, 3] + RO[g, 3].astype(f32) + RO[g, 5].astype(f32)
        SZ[g, 0] = KO[g, 2].astype(bf16)
        SZ[g, 1] = KO[g, 3].astype(bf16)
        for d in (1, 2, 3):
            z = up4(me.zl, d)
            part = pl.ds(pl.multiple_of(32 * z, 32), 32)
            zc[g, d] = push(
                SZ.at[g, pl.ds(0, 2), part], RZ.at[g, d - 1], zs.at[g, d - 1], zr.at[g, d - 1], me.tid(zl=z)
            )

    def close(g, y):
        mine = pl.ds(pl.multiple_of(32 * me.zl, 32), 32)
        for d in (1, 2, 3):
            zc[g, d].wait_recv()
        for b in range(2):
            tot = KO[g, 2 + b, mine, :]
            for d in range(3):
                tot = tot + RZ[g, d, b].astype(f32)
            outt[:, pl.ds(pl.multiple_of(256 * y + 128 * b, 128), 128)] = tot

    landed(0, 1)
    group(0, me.y)
    for p in range(4):
        hc[4, p].wait_recv()
        v = hv(0, yr, zo, p)
        move(6, p, v, yr, zo, to_l)
        share(4, p, v, yr, zo)
        hc[3, p].wait_recv()
        share(5, p, hv(0, yl, zo, p), yl, zo)
    landed(3, 4)
    group(1, yr)
    relay(0)
    landed(2, 5)
    group(2, yl)
    relay(1)
    for p in range(4):
        hc[5, p].wait_recv()
        share(6, p, hv(0, yf, zh, p), yf, zh)
    settle(0)
    for p in range(4):
        hc[6, p].wait_recv()
        share(7, p, hv(0, yf, zo, p), yf, zo)
    landed(6, 7)
    group(3, yf)
    relay(2)
    settle(1)
    relay(3)
    settle(2)
    close(0, me.y)
    settle(3)
    close(1, yr)
    close(2, yl)
    close(3, yf)
    for c in [*sent, *hc.values(), *oc.values(), *zc.values()]:
        c.wait_send()


def scales():
    low, out = 1.0 / 513.0, []
    for _ in range(8):
        out.append(2.0 / (1.0 + low))
        low = 4.0 * low / (1.0 + low) ** 2
    return out


def solve(FY, gram, coords):
    sc = scales()
    eye = lax.broadcasted_iota(jnp.int32, (NCLS, NCLS), 0) == lax.broadcasted_iota(jnp.int32, (NCLS, NCLS), 1)
    G = gram[...]
    diag = jnp.where(eye, G, 0.0)
    trace = jnp.sum(jnp.sum(diag, axis=1, keepdims=True), axis=0, keepdims=True)
    ridge = ridge_share * trace / NCLS
    inv = 1.0 / (513.0 * ridge)
    FY[:, :NCLS] = jnp.where(eye, 1.0 - sc[0] / 513.0, 0.0) - (sc[0] * inv) * G
    FY[:, NCLS:] = coords[...]

    def pick(k, vals):
        out = jnp.float32(vals[0])
        for i in range(1, len(vals)):
            out = jnp.where(k == i, jnp.float32(vals[i]), out)
        return out

    def step(k, carry):
        now, nxt = pick(k, sc[:7]), pick(k, sc[1:])
        both = jnp.dot(FY[:, :NCLS], FY[...], precision=lax.Precision.HIGHEST, preferred_element_type=f32)
        FY[:, NCLS:] = now * (FY[:, NCLS:] + both[:, NCLS:])
        FY[:, :NCLS] = nxt * both[:, :NCLS] + jnp.where(eye, 1.0 - nxt, 0.0)
        return carry

    lax.fori_loop(0, 7, step, 0)
    Y = FY[:, NCLS:]
    last = jnp.dot(FY[:, :NCLS], Y, precision=lax.Precision.HIGHEST, preferred_element_type=f32)
    return (sc[7] * inv) * (Y + last)


def stats_kernel(outt, labs, erased, gram, coords, wall, ms, rowbuf, FY,
                 zb, zg, XG, RG, SG, ZG, AG, GB, XC, RC, SC, ZC, AC,
                 ws, wr, ms_s, ms_r, as_, ar, xs, xr, gs, gr):
    me = Spot()
    other = 1 - me.core
    mate = me.dpid(core=other)
    across = me.dpid(zh=1 - me.zh)
    y_dev = [me.dpid(y=up4(me.y, d)) for d in (1, 2, 3)]
    t_dev = [{"tensor": lax.rem(me.tn + d, 16)} for d in range(1, 16)]
    greet(t_dev + y_dev + [across, mate])

    out = outt[...]
    mean = jnp.sum(out, axis=1, keepdims=True) / TOKENS
    cen = out - mean
    spread = jnp.sqrt(jnp.sum(cen * cen, axis=1, keepdims=True) / TOKENS + epsilon)
    z = cen / spread
    for j in range(8):
        zb[j] = z[:, 128 * j:128 * j + 128].astype(bf16)

    def rows32(zl, x):
        return pl.ds(pl.multiple_of(32 * (4 * x + zl), 32), 32)

    ac = []
    for d in range(1, 16):
        t = lax.rem(me.tn + d, 16)
        ac.append(push(zb.at[t // 2], zg.at[rows32(me.zl, me.x)], as_.at[d - 1], ar.at[d - 1], t_dev[d - 1]))
    zg[rows32(me.zl, me.x), :] = zb[me.tn // 2]

    cls = lax.broadcasted_iota(jnp.int32, (NCLS, 128), 0)
    c1 = cen.astype(bf16)
    r1 = cen - c1.astype(f32)
    c2 = r1.astype(bf16)
    c3 = (r1 - c2.astype(f32)).astype(bf16)
    acc = jnp.zeros((32, NCLS), f32)
    for j in range(8):
        row = labs[2 * j, 0:1, :] + labs[2 * j + 1, 0:1, :]
        hot = (cls == row).astype(f32).astype(bf16)
        cols = slice(128 * j, 128 * j + 128)
        acc = acc + nt(c1[:, cols], hot) + nt(c2[:, cols], hot) + nt(c3[:, cols], hot)
    wall[rows32(me.zl, me.x), :] = (acc / TOKENS / spread).astype(bf16)
    lane = lax.broadcasted_iota(jnp.int32, (32, 128), 1)
    slot = 4 * me.x + me.zl
    ms[slot, :, 0:32] = jnp.where(lane < 1, mean, spread).T[0:8]
    ms[slot, :, 32:] = jnp.zeros((8, 96), f32)

    def wv(zl, x):
        return wall.at[rows32(zl, x)]

    def mv(zl, x):
        return ms.at[4 * x + zl]

    sent = gather_tensor(
        me, [(wv(me.zl, me.x), wv, ws, wr), (mv(me.zl, me.x), mv, ms_s, ms_r)]
    )
    for c in ac:
        c.wait_recv()
    sent += ac
    zz = zg[...].astype(f32)
    zz = jnp.where(lax.rem(me.tn, 2) == 1, pltpu.roll(zz, 64, 1), zz)
    zall = zz.astype(bf16)
    wt = wall[...].T
    G = jnp.dot(wt, wall[...], preferred_element_type=f32)
    C = jnp.dot(wt, zall, preferred_element_type=f32)
    gram[...] = G
    lane = lax.broadcasted_iota(jnp.int32, (128, 128), 1)
    XC[...] = jnp.where(lane < 64, C[:128], pltpu.roll(C[128:], 64, 1))
    mine = pl.ds(pl.multiple_of(16 * me.tn, 16), 16)
    XG[0:16, :] = gram[mine, 0:128]
    XG[16:32, :] = gram[mine, 128:256]
    chains = ((16, XG, RG, SG, ZG, AG, GB.at[me.tn]), (64, XC, RC, SC, ZC, AC, coords))

    def half(n, c):
        return pl.ds(pl.multiple_of(n * c, 8), n)

    cp = {}
    for i, (n, X, R, *_) in enumerate(chains):
        cp[i, 0] = push(X.at[half(n, other)], R, xs.at[i, 0], xr.at[i, 0], mate)
    for i, (n, X, R, SS, Z, *_) in enumerate(chains):
        cp[i, 0].wait_recv()
        SS[...] = X[half(n, me.core), :] + R[...]
        cp[i, 1] = push(SS, Z, xs.at[i, 1], xr.at[i, 1], across)
    for i, (n, _, _, SS, Z, A, _) in enumerate(chains):
        cp[i, 1].wait_recv()
        A[me.y] = SS[...] + Z[...]
        for k, dev in enumerate(y_dev):
            cp[i, 2 + k] = push(A.at[me.y], A.at[me.y], xs.at[i, 2 + k], xr.at[i, 2 + k], dev)

    def finish(i):
        n, A, out = chains[i][0], chains[i][5], chains[i][6]
        for k in range(3):
            cp[i, 2 + k].wait_recv()
        own = half(n, me.core)
        out[own, :] = A[0] + A[1] + A[2] + A[3]
        cp[i, 5] = push(out.at[own], out.at[own], xs.at[i, 5], xr.at[i, 5], mate)

    def gv(zl, x):
        return GB.at[4 * zl + x]

    finish(0)
    cp[0, 5].wait_recv()
    sent += gather_tensor(me, [(gv(me.zl, me.x), gv, gs, gr)])
    finish(1)
    for t in range(16):
        gram[16 * t:16 * t + 16, 0:128] = GB[t, 0:16, :]
        gram[16 * t:16 * t + 16, 128:256] = GB[t, 16:32, :]
        rowbuf[:, 32 * t:32 * t + 32] = ms[t, :, 0:32]
    cp[1, 5].wait_recv()
    coords[128:256, :] = pltpu.roll(coords[0:128, :], 64, 1)
    solved = solve(FY, gram, coords)
    fix = jnp.dot(wall[...], solved.astype(bf16), preferred_element_type=f32)
    rest = (zz - fix).T[:64]
    erased[...] = (rowbuf[0:1, :] + rowbuf[1:2, :] * rest).astype(bf16)
    for c in [*sent, *cp.values()]:
        c.wait_send()


def params(cid):
    return pltpu.CompilerParams(collective_id=cid, has_side_effects=True, vmem_limit_bytes=56 * 2**20)


DMA = pltpu.SemaphoreType.DMA
V = pltpu.VMEM
S = jax.ShapeDtypeStruct


def shards(tokens, gate_weight, up_weight, down_weight, labels):
    tn = lax.axis_index("tensor")
    twice = jnp.concatenate([labels, labels])[None, :]
    keep = (jnp.arange(128) // 64)[None, :] == tn % 2
    lab = jnp.broadcast_to(jnp.where(keep, twice, 0), (8, 128))
    nq = len(CHUNKS)
    h, labs = pl.pallas_call(
        hidden_kernel,
        out_shape=(S((UNITS, 128), bf16), S((16, 8, 128), jnp.int32)),
        in_specs=[VM, VM, ANY, ANY],
        out_specs=(VM, VM),
        scratch_shapes=[
            V((1024, 512), bf16), V((1024, 512), bf16), V((2, 2, UNITS, 512), bf16),
            V((6, 2 * UNITS, 128), bf16), V((6, 2 * UNITS, 128), bf16), V((2, 2 * UNITS, 128), f32),
            V((2 * UNITS, 256), f32), V((2 * UNITS, 128), bf16), V((2 * UNITS, 128), bf16),
            DMA((16,)), DMA((16,)), DMA((16,)), DMA((16,)), DMA((2,)), DMA((2,)), DMA((2,)),
            DMA((4,)), DMA((4,)), DMA((6, nq)), DMA((6, nq)), DMA((nq,)), DMA((nq,)),
        ],
        compiler_params=params(0),
        name="gate_up_hidden",
    )(tokens, lab, gate_weight.T, up_weight.T)
    outt = pl.pallas_call(
        down_kernel,
        out_shape=S((32, 1024), f32),
        in_specs=[VM, ANY],
        out_specs=VM,
        scratch_shapes=[
            V((2, 1024, 512), bf16), V((2, 512, 1024), bf16), V((2, 4, 1024, 256), bf16),
            V((512, 256), f32), V((4, 4, 128, 128), f32), V((4, 6, 128, 128), bf16),
            V((4, 6, 128, 128), bf16), V((4, 2, 128, 128), bf16), V((4, 3, 2, 32, 128), bf16),
            DMA((2,)), DMA((7, 4)), DMA((7, 4)), DMA((8, 4)), DMA((8, 4)),
            DMA((4, 6)), DMA((4, 6)), DMA((4, 3)), DMA((4, 3)),
        ],
        compiler_params=params(1),
        name="down_scatter",
    )(h, down_weight)
    return pl.pallas_call(
        stats_kernel,
        out_shape=S((64, 512), bf16),
        in_specs=[VM, VM],
        out_specs=VM,
        scratch_shapes=[
            V((256, 256), f32), V((256, 128), f32), V((512, 256), bf16), V((16, 8, 128), f32), V((8, 512), f32),
            V((256, 384), f32), V((8, 32, 128), bf16), V((512, 128), bf16),
            V((32, 128), f32), V((16, 128), f32), V((16, 128), f32), V((16, 128), f32), V((4, 16, 128), f32),
            V((16, 32, 128), f32),
            V((128, 128), f32), V((64, 128), f32), V((64, 128), f32), V((64, 128), f32), V((4, 64, 128), f32),
            DMA((16,)), DMA((16,)), DMA((16,)), DMA((16,)), DMA((15,)), DMA((15,)),
            DMA((2, 6)), DMA((2, 6)), DMA((16,)), DMA((16,)),
        ],
        compiler_params=params(2),
        name="stats_solve_erase",
    )(outt, labs)


def solution(mesh):
    return jax.shard_map(
        shards,
        mesh=mesh,
        in_specs=(
            P("tensor", "dp"),
            P("dp", "tensor"),
            P("dp", "tensor"),
            P("tensor", "dp"),
            P("tensor"),
        ),
        out_specs=P("tensor", "dp"),
        check_vma=False,
    )
```
